32 devices in a mesh: blk: 8 (over z, x), ch: 4 (over y, core).
Axes of the slice: x: 2, y: 2, z: 4, core: 2. Of those that a mesh axis runs over, the one named last changes fastest.
Arguments:
- features: bfloat16 [128, 128, 512], P('blk', 'ch'), may hold values from -6 to 6
- weights: bfloat16 [27, 128, 128], P(None, 'ch'), may hold values from -0.109375 to 0.109375
- bias: float32 [128], P('ch'), may hold values from -3 to 3
- occupancy: int32 [128, 512], P('blk'), may hold values 0 or 1
- live: int32 [8], P('blk'), may hold values from 1 to 16, as said below
- neighbours: int32 [128, 3, 2], replicated, may hold values from 0 to 127, as said below
Outputs:
- convolved: bfloat16 [128, 128, 512], P('blk', 'ch')
The draws below stay inside these ranges and needn't reach their ends.
Inputs may be any that keep to these rules, and one draw needn't show every extreme that they name: Each device's first live[d] slots are live; some device has all 16 slots live. Along each dimension d, b -> neighbours[b, d, 0] is a one-to-one map of all blocks, and neighbours[b, d, 1] is its inverse. Along each dimension, the upper neighbours of one device's blocks lie on 4 devices, exactly 4 on each.
All inputs are finite; a program needn't handle non-finite values. No bound on the sum of `occupancy` on one device may be relied on, other than what follows from the above.
Results may differ from the reference program's by a relative error of at most 0.003.
Values may be sent and summed in bfloat16 or wider, within the bound.
No kernel may reach another device: no remote copies, remote signals or barrier semaphores. Data moves between devices by JAX's collectives and lax.ppermute only.
A program may use at most 192 MiB of HBM per device.

```python
import jax
import jax.numpy as jnp
from jax import lax

C = 128
BLK_DEV = 16
GROUP = 4
BLOCKS = 128
N_BLK = 8


def draw_live(key, part):
    raw_draw = jax.random.randint(jax.random.fold_in(key, 5), (N_BLK,), 0, BLK_DEV)
    counts_live = 1 + raw_draw * raw_draw // BLK_DEV
    chosen = jax.random.randint(jax.random.fold_in(key, 6), (), 0, N_BLK)
    return counts_live.at[chosen].set(BLK_DEV).astype(jnp.int32)


def shuffled_slots(subkey):
    return jax.random.permutation(subkey, BLK_DEV)


def draw_neighbours(key, part):
    columns = []
    for direction in range(3):
        branch = jax.random.fold_in(key, 11 + direction)
        keys_all = jax.random.split(branch, 4)
        spread = jax.random.permutation(keys_all[0], N_BLK)
        relabel = jax.random.permutation(keys_all[1], N_BLK)
        offsets = jax.random.permutation(keys_all[2], N_BLK)[:BLK_DEV // GROUP]
        slot_order = jax.vmap(shuffled_slots)(jax.random.split(keys_all[3], N_BLK))
        bucket = slot_order // GROUP
        target_dev = relabel[(spread[:, None] + offsets[bucket]) % N_BLK]
        upward = (target_dev * BLK_DEV + slot_order).reshape(-1).astype(jnp.int32)
        downward = jnp.zeros((N_BLK * BLK_DEV,), jnp.int32).at[upward].set(jnp.arange(N_BLK * BLK_DEV, dtype=jnp.int32))
        columns.append(jnp.stack([upward, downward], axis=-1))
    return jnp.stack(columns, axis=1)


def set_ends(drawn, stream_key, least, largest):
    extent = drawn.shape
    place = [jax.random.randint(jax.random.fold_in(stream_key, axis), (), 0, extent[axis]) for axis in range(len(extent))]
    drawn = drawn.at[tuple(place)].set(least)
    longest = extent.index(max(extent))
    place[longest] = (place[longest] + 1) % extent[longest]
    return drawn.at[tuple(place)].set(largest)


def level_of(rng, extent, cuts, least, high):
    def one(axis_at, blocks):
        steps = jax.random.uniform(jax.random.fold_in(jax.random.fold_in(rng, 6), axis_at), (blocks,), jnp.float32, least / len(cuts), high / len(cuts))
        return jnp.repeat(jnp.exp(steps), extent[axis_at] // blocks).reshape((-1,) + (1,) * (len(extent) - axis_at - 1))

    level = one(*cuts[0])
    for cut in cuts[1:]:
        level = level * one(*cut)
    return level


def gaussian(own_key, extent, scale, limit, pieces=(), held_as=jnp.bfloat16):
    loudness = level_of(own_key, extent, pieces, -0.22, 0.18) if pieces else 1.0
    entries = jax.random.normal(own_key, extent, jnp.float32) * scale * loudness
    return jnp.minimum(jnp.maximum(entries, -limit), limit).astype(held_as)


def setup_inputs(seed: int = 0) -> dict:
    seeds = jax.random.split(jax.random.key(seed), 7)
    return {
        "features": gaussian(seeds[0], (BLOCKS, C, 512), 1.0, 6.0, ((0, 8), (1, 4))),
        "weights": gaussian(seeds[1], (27, C, C), (27 * C) ** -0.5, 0.109375, ((1, 4),)),
        "bias": gaussian(seeds[2], (C,), 0.5, 3.0, ((0, 4),), jnp.float32),
        "occupancy": set_ends((jax.random.randint(seeds[3], (BLOCKS, 512), 0, 2) < 1).astype(jnp.int32), jax.random.fold_in(seeds[3], 1), 0, 1),
        "live": draw_live(jax.random.fold_in(seeds[6], 71), 0),
        "neighbours": draw_neighbours(jax.random.fold_in(seeds[6], 71), 0),
    }


OFFSETS = [(shift_i, shift_j, shift_k) for shift_i in (-1, 0, 1) for shift_j in (-1, 0, 1) for shift_k in (-1, 0, 1)]


def place_partials(products):
    batch_size = products.shape[0]
    channels_out = products.shape[2]
    cubes = products.reshape(batch_size, 27, channels_out, 8, 8, 8)
    padded_sum = jnp.zeros((batch_size, channels_out, 10, 10, 10), jnp.float32)
    for offset, (shift_i, shift_j, shift_k) in enumerate(OFFSETS):
        widths = ((0, 0), (0, 0), (1 - shift_i, 1 + shift_i), (1 - shift_j, 1 + shift_j), (1 - shift_k, 1 + shift_k))
        padded_sum = padded_sum + jnp.pad(cubes[:, offset], widths)
    return padded_sum


def reference(features, weights, bias, occupancy, live, neighbours):
    total_blocks = features.shape[0]
    slot_ids = jnp.arange(total_blocks, dtype=jnp.int32) % BLK_DEV
    owner_ids = jnp.arange(total_blocks, dtype=jnp.int32) // BLK_DEV
    active = occupancy * (slot_ids < live[owner_ids]).astype(jnp.int32)[:, None]
    masked = features * active[:, None, :].astype(jnp.bfloat16)
    group_width = 16 if C % 16 == 0 else C
    groups = C // group_width
    batch_rows = 128 if total_blocks % 128 == 0 else total_blocks
    batched = masked.reshape(total_blocks // batch_rows, batch_rows, C, 512)

    def one_group(group_index):
        w_group = lax.dynamic_slice_in_dim(weights, group_index * group_width, group_width, 1).astype(jnp.float32)

        def one_batch(block_rows):
            products = jnp.einsum("ock,bkv->bocv", w_group, block_rows.astype(jnp.float32))
            return place_partials(products)

        volume = lax.map(one_batch, batched).reshape(total_blocks, group_width, 10, 10, 10)
        for direction in range(3):
            upper_face = volume[:, :, -1]
            lower_face = volume[:, :, 0]
            interior = volume[:, :, 1:-1]
            from_below = jnp.zeros_like(upper_face).at[neighbours[:, direction, 0]].add(upper_face)
            from_above = jnp.zeros_like(lower_face).at[neighbours[:, direction, 1]].add(lower_face)
            interior = interior.at[:, :, 0].add(from_below).at[:, :, -1].add(from_above)
            volume = jnp.moveaxis(interior, 2, 4)
        summed = volume.reshape(total_blocks, group_width, 512)
        gains = lax.dynamic_slice_in_dim(bias, group_index * group_width, group_width, 0)
        result = (summed + gains[None, :, None]) * active[:, None, :].astype(jnp.float32)
        return result.astype(jnp.bfloat16)

    stacked = lax.map(one_group, jnp.arange(groups, dtype=jnp.int32))
    return jnp.transpose(stacked, (1, 0, 2, 3)).reshape(total_blocks, C, 512)
```

```python
import functools

import jax
import jax.numpy as jnp
import numpy as np
from jax import lax
from jax.experimental import pallas as pl
from jax.experimental.pallas import tpu as pltpu
from jax.sharding import PartitionSpec as P

SIDE = 8
PAD = SIDE + 2
LANES = 128
HALF = SIDE * SIDE
VMEM_LIMIT = 56 * 1024 * 1024

FACES = [(1, 0), (1, 1), (2, 0), (2, 1)]
EDGES = [(0, 0), (0, 1), (1, 0), (1, 1)]


def outer(q):
    return PAD - 1 if q == 0 else 0


def inner(q):
    return 1 if q == 0 else SIDE


@functools.lru_cache(None)
def tables():
    expand = np.zeros((LANES, 2 * LANES), np.float32)
    for a in range(2):
        for j in range(SIDE):
            for k in range(SIDE):
                expand[a * HALF + j * SIDE + k, a * LANES + (j + 1) * PAD + k + 1] = 1
    gather = np.zeros((SIDE * LANES, 3 * LANES), np.float32)
    scatter = np.zeros((3 * LANES, SIDE * LANES), np.float32)
    for i in range(SIDE):
        for d, q in FACES:
            for a in range(SIDE):
                lane = (d - 1) * LANES + (1 - q) * HALF + i * SIDE + a
                if d == 1:
                    source, target = outer(q) * PAD + a + 1, inner(q) * PAD + a + 1
                else:
                    source, target = (a + 1) * PAD + outer(q), (a + 1) * PAD + inner(q)
                gather[i * LANES + source, lane] = 1
                scatter[lane, i * LANES + target] = 1
        for e, (qj, qk) in enumerate(EDGES):
            lane = 2 * LANES + e * SIDE + i
            gather[i * LANES + outer(qj) * PAD + outer(qk), lane] = 1
            scatter[lane, i * LANES + inner(qj) * PAD + inner(qk)] = 1
    return expand, gather, scatter


def div(value, size):
    return value >> (size.bit_length() - 1) if size & (size - 1) == 0 else lax.div(value, size)


def mod(value, size):
    return value & (size - 1) if size & (size - 1) == 0 else lax.rem(value, size)


def popcount(x):
    x = x - ((x >> 1) & 0x55555555)
    x = (x & 0x33333333) + ((x >> 2) & 0x33333333)
    x = (x + (x >> 4)) & 0x0F0F0F0F
    x = x + (x >> 8)
    return (x + (x >> 16)) & 0x3F


def clear(ref, size):
    def step(n, _):
        ref[n] = 0
        return 0

    lax.fori_loop(0, size, step, 0)


def slot_of(kind, peer, place, cap, slots):
    rows = 2 * cap + slots // 4
    if kind < 4:
        return peer * rows + (FACES[kind][0] - 1) * cap + place
    if kind < 8:
        return (peer * rows + 2 * cap) * 4 + place
    return peer * cap + place


def table_kernel(peers, cap, slots, me_ref, nbr, send, recv, count, mask):
    me = me_ref[0]
    first = me * slots
    clear(count, 8 * peers)
    clear(mask, 10 * peers)

    def dest(b, kind):
        if kind < 4:
            d, q = FACES[kind]
            return nbr[b * 6 + 2 * d + q]
        qj, qk = EDGES[kind - 4]
        return nbr[nbr[b * 6 + 2 + qj] * 6 + 4 + qk]

    def source(r, kind):
        if kind >= 8:
            return nbr[r * 6 + 1 - (kind - 8)]
        if kind < 4:
            d, q = FACES[kind]
            return nbr[r * 6 + 2 * d + 1 - q]
        qj, qk = EDGES[kind - 4]
        return nbr[nbr[r * 6 + 4 + 1 - qk] * 6 + 2 + 1 - qj]

    def gather(s, _):
        for kind in range(8):
            peer = div(dest(first + s, kind), slots)
            place = count[kind * peers + peer]
            count[kind * peers + peer] = place + 1
            send[kind * slots + s] = slot_of(kind, peer, place, cap, slots)
        for kind in range(10):
            b = source(first + s, kind)
            at = kind * peers + div(b, slots)
            mask[at] = mask[at] | (1 << mod(b, slots))
        return 0

    lax.fori_loop(0, slots, gather, 0)

    def rank(r, _):
        for kind in range(10):
            b = source(first + r, kind)
            peer = div(b, slots)
            before = popcount(mask[kind * peers + peer] & ((1 << mod(b, slots)) - 1))
            recv[kind * slots + r] = slot_of(kind, peer, before, cap, slots)
        return 0

    lax.fori_loop(0, slots, rank, 0)


def active_row(occ_ref, s, live):
    return occ_ref[pl.ds(s, 1), :].astype(jnp.float32) * (s < live).astype(jnp.float32)


def pack_kernel(peers, cap, slots, me_ref, live_ref, nbr, occ, low, high, out, count):
    first = me_ref[0] * slots
    live = live_ref[0]
    clear(count, 2 * peers)
    for s in range(slots):
        row = active_row(occ, s, live).astype(jnp.bfloat16)
        for q in range(2):
            peer = div(nbr[(first + s) * 6 + q], slots)
            place = count[q * peers + peer]
            count[q * peers + peer] = place + 1
            half = slice(0, HALF) if q == 1 else slice(HALF, LANES)
            face = low if q == 1 else high
            lanes = row[:, :LANES] if q == 1 else row[:, -LANES:]
            out[peer * cap + place, :, half] = (face[s] * lanes)[:, half]


def order_kernel(slots, recv, arrived, out):
    lane = lax.broadcasted_iota(jnp.int32, arrived.shape[1:], 1)
    for r in range(slots):
        up = arrived[recv[8 * slots + r]]
        down = arrived[recv[9 * slots + r]]
        out[r] = jnp.where(lane < HALF, down, up)


def conv_kernel(
    keys, slots, cap, group, me_ref, live_ref, send, occ, weights, expand, gather, *refs
):
    n = len(keys)
    xs, hs = refs[:n], refs[n : 2 * n]
    out, faces = refs[2 * n : 2 * n + 2]
    wide, rows, stack, prod, packed = refs[2 * n + 2 :]
    channels = weights.shape[1]
    every = weights.shape[2]
    step = pl.program_id(0)
    me = me_ref[0]
    live = live_ref[0]

    @pl.when(step == 0)
    def _():
        for g in range(9):
            for r in range(3):
                wide[g * channels : (g + 1) * channels, r * every : (r + 1) * every] = weights[3 * g + r]

    def block(b, _):
        s = step * group + b
        row = active_row(occ, s, live).astype(jnp.bfloat16)
        for key, x, h in zip(keys, xs, hs):
            at = pl.multiple_of((me ^ key) * channels, channels)
            masked = x[b] * row
            for v in range(4):
                rows[v, pl.ds(at, channels), :] = masked[:, v * LANES : (v + 1) * LANES]
            rows[4, pl.ds(at, channels), :] = h[b]
        for v in range(5):
            planes = jnp.dot(rows[v], expand[...], preferred_element_type=jnp.float32)
            for a in range(2):
                layer = 2 * v + 1 + a if v < 4 else 9 * (1 - a)
                at = slice(layer * LANES, (layer + 1) * LANES)
                plane = planes[:, a * LANES : (a + 1) * LANES]
                stack[0:every, at] = pltpu.roll(plane, 1, axis=1).astype(jnp.bfloat16)
                stack[every : 2 * every, at] = plane.astype(jnp.bfloat16)
                stack[2 * every : 3 * every, at] = pltpu.roll(plane, LANES - 1, axis=1).astype(jnp.bfloat16)
        prod[...] = jnp.dot(wide[...], stack[...], preferred_element_type=jnp.float32)
        for layer in range(SIDE):
            at = slice(layer * LANES, (layer + 1) * LANES)
            sums = []
            for q in range(3):
                total = None
                for p in range(3):
                    first = (3 * p + q) * channels
                    part = prod[first : first + channels, (layer + p) * LANES : (layer + p + 1) * LANES]
                    total = part if total is None else total + part
                sums.append(total)
            result = sums[1] + pltpu.roll(sums[0], PAD, axis=1) + pltpu.roll(sums[2], LANES - PAD, axis=1)
            out[b, :, at] = result
            packed[b, :, at] = result.astype(jnp.bfloat16)

        return 0

    lax.fori_loop(0, group, block, 0)
    shell = jnp.dot(
        packed[...].reshape(group * channels, SIDE * LANES), gather[...], preferred_element_type=jnp.float32
    )
    lane = lax.broadcasted_iota(jnp.int32, (channels, LANES), 1)
    for b in range(group):
        s = step * group + b
        mine = shell[b * channels : (b + 1) * channels]
        for d in range(2):
            pair = mine[:, d * LANES : (d + 1) * LANES].astype(jnp.bfloat16)
            faces[send[(2 * d + 1) * slots + s], :, :HALF] = pair[:, :HALF]
            faces[send[2 * d * slots + s], :, HALF:] = pair[:, HALF:]
        edge = mine[:, 2 * LANES :]
        for e in range(4):
            slot = send[(4 + e) * slots + s]
            shift = (slot & 3) * 32
            moved = pltpu.roll(edge, shift, axis=1).astype(jnp.bfloat16)
            keep = jnp.logical_and(lane >= shift + e * SIDE, lane < shift + (e + 1) * SIDE)
            faces[slot >> 2] = jnp.where(keep, moved, faces[slot >> 2])


def final_kernel(slots, recv, live_ref, occ, bias, scatter, squeeze, base, faces, out, shell):
    channels = base.shape[1]
    live = live_ref[0]
    lane = lax.broadcasted_iota(jnp.int32, (channels, LANES), 1)
    for r in range(slots):
        for d in range(2):
            up = faces[recv[2 * d * slots + r]]
            down = faces[recv[(2 * d + 1) * slots + r]]
            shell[r, :, d * LANES : (d + 1) * LANES] = jnp.where(lane < HALF, down, up)
        total = jnp.zeros((channels, LANES), jnp.float32)
        for e in range(4):
            slot = recv[(4 + e) * slots + r]
            moved = pltpu.roll(faces[slot >> 2].astype(jnp.float32), (LANES - (slot & 3) * 32) & (LANES - 1), axis=1)
            keep = jnp.logical_and(lane >= e * SIDE, lane < (e + 1) * SIDE)
            total = jnp.where(keep, moved, total)
        shell[r, :, 2 * LANES :] = total.astype(jnp.bfloat16)
    added = jnp.dot(
        shell[...].reshape(slots * channels, 3 * LANES), scatter[...], preferred_element_type=jnp.float32
    )
    for r in range(slots):
        summed = base[r] + added[r * channels : (r + 1) * channels] + bias[...]
        rounded = summed.astype(jnp.bfloat16)
        row = active_row(occ, r, live).astype(jnp.bfloat16)
        for v in range(4):
            pair = rounded[:, 2 * v * LANES : 2 * (v + 1) * LANES]
            at = slice(v * LANES, (v + 1) * LANES)
            flat = jnp.dot(pair, squeeze[...], preferred_element_type=jnp.float32).astype(jnp.bfloat16)
            out[r, :, at] = flat * row[:, at]


def spread(x, axis, size):
    have = {0: x}
    bit = size >> 1
    while bit:
        for key in list(have):
            have[key ^ bit] = lax.ppermute(have[key], axis, [(n, n ^ bit) for n in range(size)])
        bit >>= 1
    return have


def shards(features, weights, bias, occupancy, live, neighbours):
    slots, channels, voxels = features.shape
    peers = lax.axis_size("blk")
    members = lax.axis_size("ch")
    cap = max(2, 2 * slots // peers)
    every = channels * members
    group = 4
    bf16, f32, i32 = jnp.bfloat16, jnp.float32, jnp.int32
    smem = pl.BlockSpec(memory_space=pltpu.SMEM)
    vmem = pl.BlockSpec(memory_space=pltpu.VMEM)
    params = pltpu.CompilerParams(vmem_limit_bytes=VMEM_LIMIT)
    expand, gather, scatter = (jnp.asarray(t, bf16) for t in tables())
    squeeze = expand.T
    place = lax.axis_index("blk").astype(i32).reshape(1)
    member = lax.axis_index("ch").astype(i32).reshape(1)
    nbr = neighbours.reshape(-1)

    have = spread(features, "ch", members)

    corner = pl.BlockSpec((slots, channels, LANES), lambda n: (0, 0, 0))
    corner_last = pl.BlockSpec((slots, channels, LANES), lambda n: (0, 0, voxels // LANES - 1))
    outgoing = pl.pallas_call(
        functools.partial(pack_kernel, peers, cap, slots),
        grid=(1,),
        out_shape=jax.ShapeDtypeStruct((peers * cap, channels, LANES), bf16),
        in_specs=[smem, smem, smem, vmem, corner, corner_last],
        out_specs=vmem,
        scratch_shapes=[pltpu.SMEM((2 * peers,), i32)],
        compiler_params=params,
        name="pack_layers",
    )(place, live, nbr, occupancy, features, features)
    arrived = lax.all_to_all(outgoing, "blk", split_axis=0, concat_axis=0, tiled=True)

    send, recv = pl.pallas_call(
        functools.partial(table_kernel, peers, cap, slots),
        out_shape=(jax.ShapeDtypeStruct((8 * slots,), i32), jax.ShapeDtypeStruct((10 * slots,), i32)),
        in_specs=[smem, smem],
        out_specs=(smem, smem),
        scratch_shapes=[pltpu.SMEM((8 * peers,), i32), pltpu.SMEM((10 * peers,), i32)],
        name="slot_tables",
    )(place, nbr)

    layers = pl.pallas_call(
        functools.partial(order_kernel, slots),
        out_shape=jax.ShapeDtypeStruct((slots, channels, LANES), bf16),
        in_specs=[smem, vmem],
        out_specs=vmem,
        compiler_params=params,
        name="order_layers",
    )(recv, arrived)
    halo = spread(layers, "ch", members)

    keys = sorted(have)
    own = pl.BlockSpec((group, channels, voxels), lambda n: (n, 0, 0))
    own_halo = pl.BlockSpec((group, channels, LANES), lambda n: (n, 0, 0))
    base, faces = pl.pallas_call(
        functools.partial(conv_kernel, keys, slots, cap, group),
        grid=(slots // group,),
        out_shape=(
            jax.ShapeDtypeStruct((slots, channels, SIDE * LANES), f32),
            jax.ShapeDtypeStruct((peers * (2 * cap + slots // 4), channels, LANES), bf16),
        ),
        in_specs=[smem, smem, smem, vmem, vmem, vmem, vmem] + [own] * len(keys) + [own_halo] * len(keys),
        out_specs=(pl.BlockSpec((group, channels, SIDE * LANES), lambda n: (n, 0, 0)), vmem),
        scratch_shapes=[
            pltpu.VMEM((9 * channels, 3 * every), bf16),
            pltpu.VMEM((5, every, LANES), bf16),
            pltpu.VMEM((3 * every, PAD * LANES), bf16),
            pltpu.VMEM((9 * channels, PAD * LANES), f32),
            pltpu.VMEM((group, channels, SIDE * LANES), bf16),
        ],
        compiler_params=params,
        name="convolve",
    )(member, live, send, occupancy, weights, expand, gather, *[have[k] for k in keys], *[halo[k] for k in keys])

    faces = lax.all_to_all(faces, "blk", split_axis=0, concat_axis=0, tiled=True)

    return pl.pallas_call(
        functools.partial(final_kernel, slots),
        out_shape=jax.ShapeDtypeStruct((slots, channels, voxels), bf16),
        in_specs=[smem, smem] + [vmem] * 6,
        out_specs=vmem,
        scratch_shapes=[pltpu.VMEM((slots, channels, 3 * LANES), bf16)],
        compiler_params=params,
        name="finish",
    )(recv, live, occupancy, bias[:, None], scatter, squeeze, base, faces)


def solution(mesh):
    in_specs = (P("blk", "ch", None), P(None, "ch", None), P("ch"), P("blk", None), P("blk"), P())
    out_specs = P("blk", "ch", None)
    return jax.shard_map(shards, mesh=mesh, in_specs=in_specs, out_specs=out_specs, check_vma=False)
```

```python
import functools

import jax
import jax.numpy as jnp
import numpy as np
from jax import lax
from jax.experimental import pallas as pl
from jax.experimental.pallas import tpu as pltpu
from jax.sharding import PartitionSpec as P

SIDE = 8
PAD = SIDE + 2
LANES = 128
HALF = SIDE * SIDE
VMEM_LIMIT = 57 * 1024 * 1024

FACES = [(1, 0), (1, 1), (2, 0), (2, 1)]
EDGES = [(0, 0), (0, 1), (1, 0), (1, 1)]


def outer(q):
    return PAD - 1 if q == 0 else 0


def inner(q):
    return 0 if q == 0 else SIDE - 1


@functools.lru_cache(None)
def tables():
    expand = np.zeros((LANES, 2 * LANES), np.float32)
    for a in range(2):
        for j in range(SIDE):
            for k in range(SIDE):
                expand[a * HALF + j * SIDE + k, a * LANES + (j + 1) * PAD + k + 1] = 1
    gather = np.zeros((SIDE * LANES, 3 * LANES), np.float32)
    scatter = np.zeros((3 * LANES, SIDE * HALF), np.float32)
    for i in range(SIDE):
        for d, q in FACES:
            for a in range(SIDE):
                lane = (d - 1) * LANES + (1 - q) * HALF + i * SIDE + a
                if d == 1:
                    source, target = outer(q) * PAD + a + 1, inner(q) * SIDE + a
                else:
                    source, target = (a + 1) * PAD + outer(q), a * SIDE + inner(q)
                gather[i * LANES + source, lane] = 1
                scatter[lane, i * HALF + target] = 1
        for quarter in range(4):
            for e, (qj, qk) in enumerate(EDGES):
                lane = 2 * LANES + quarter * 4 * SIDE + e * SIDE + i
                gather[i * LANES + outer(qj) * PAD + outer(qk), lane] = 1
                scatter[lane, i * HALF + inner(qj) * SIDE + inner(qk)] = 1
    return expand, gather, scatter


def div(value, size):
    return value >> (size.bit_length() - 1) if size & (size - 1) == 0 else lax.div(value, size)


def mod(value, size):
    return value & (size - 1) if size & (size - 1) == 0 else lax.rem(value, size)


def popcount(x):
    x = x - ((x >> 1) & 0x55555555)
    x = (x & 0x33333333) + ((x >> 2) & 0x33333333)
    x = (x + (x >> 4)) & 0x0F0F0F0F
    x = x + (x >> 8)
    return (x + (x >> 16)) & 0x3F


def clear(ref, size):
    def step(n, _):
        ref[n] = 0
        return 0

    lax.fori_loop(0, size, step, 0)


def slot_of(kind, peer, place, cap, slots):
    rows = 2 * cap + slots // 4
    if kind < 4:
        return peer * rows + (FACES[kind][0] - 1) * cap + place
    if kind < 8:
        return (peer * rows + 2 * cap) * 4 + place
    return peer * cap + place


def neighbour(nbr, b, d, q):
    return nbr[d, q, b]


def dest(nbr, b, kind):
    if kind < 4:
        return neighbour(nbr, b, *FACES[kind])
    qj, qk = EDGES[kind - 4]
    return neighbour(nbr, neighbour(nbr, b, 1, qj), 2, qk)


def source(nbr, r, kind):
    if kind >= 8:
        return neighbour(nbr, r, 0, 1 - (kind - 8))
    if kind < 4:
        d, q = FACES[kind]
        return neighbour(nbr, r, d, 1 - q)
    qj, qk = EDGES[kind - 4]
    return neighbour(nbr, neighbour(nbr, r, 2, 1 - qk), 1, 1 - qj)


def send_kernel(peers, cap, slots, me_ref, nbr, send, count):
    first = me_ref[0] * slots
    clear(count, 8 * peers)

    def place_of(s, _):
        for kind in range(8):
            peer = div(dest(nbr, first + s, kind), slots)
            place = count[kind * peers + peer]
            count[kind * peers + peer] = place + 1
            send[kind * slots + s] = slot_of(kind, peer, place, cap, slots) if kind < 4 else peer * slots + place
        return 0

    lax.fori_loop(0, slots, place_of, 0)


def table_kernel(kinds, peers, cap, slots, me_ref, nbr, recv, mask):
    first = me_ref[0] * slots
    clear(mask, len(kinds) * peers)

    def gather(s, _):
        for n, kind in enumerate(kinds):
            b = source(nbr, first + s, kind)
            at = n * peers + div(b, slots)
            mask[at] = mask[at] | (1 << mod(b, slots))
        return 0

    lax.fori_loop(0, slots, gather, 0)

    def rank(r, _):
        for n, kind in enumerate(kinds):
            b = source(nbr, first + r, kind)
            peer = div(b, slots)
            before = popcount(mask[n * peers + peer] & ((1 << mod(b, slots)) - 1))
            recv[n * slots + r] = slot_of(kind, peer, before, cap, slots)
        return 0

    lax.fori_loop(0, slots, rank, 0)


def early_kernel(peers, cap, slots, me_ref, nbr, send, recv, count, mask):
    send_kernel(peers, cap, slots, me_ref, nbr, send, count)
    table_kernel((8, 9), peers, cap, slots, me_ref, nbr, recv, mask)


def active_row(occ_ref, s, live):
    return occ_ref[pl.ds(s, 1), :].astype(jnp.float32) * (s < live).astype(jnp.float32)


def pack_kernel(peers, cap, slots, me_ref, live_ref, nbr, occ, low, high, out, count):
    first = me_ref[0] * slots
    live = live_ref[0]
    clear(count, 2 * peers)
    for s in range(slots):
        row = active_row(occ, s, live).astype(jnp.bfloat16)
        for q in range(2):
            peer = div(neighbour(nbr, first + s, 0, q), slots)
            place = count[q * peers + peer]
            count[q * peers + peer] = place + 1
            half = slice(0, HALF) if q == 1 else slice(HALF, LANES)
            face = low if q == 1 else high
            lanes = row[:, :LANES] if q == 1 else row[:, -LANES:]
            out[peer * cap + place, :, half] = (face[s] * lanes)[:, half]


def order_kernel(slots, recv, arrived, out):
    lane = lax.broadcasted_iota(jnp.int32, arrived.shape[1:], 1)
    for r in range(slots):
        up = arrived[recv[r]]
        down = arrived[recv[slots + r]]
        out[r] = jnp.where(lane < HALF, down, up)


def shifted(plane, by):
    return pltpu.roll(plane, by % LANES, axis=1)


def half_weights(weights, wide, upper):
    channels, every = weights.shape[1:]
    half = every // 2
    for g in range(9):
        for r in range(3):
            w = weights[3 * g + r]
            wide[g * channels : (g + 1) * channels, r * half : (r + 1) * half] = jnp.where(
                upper, w[:, half:], w[:, :half]
            )


def conv_blocks(blocks, sets, wide, expand):
    channels = wide.shape[0] // 9
    for (row, parts), (rows, stack, prod) in zip(blocks, sets):
        size = rows.shape[0] // 4
        for at, x in parts:
            masked = x * row
            for v in range(4):
                here = pl.multiple_of(v * size + at, channels)
                rows[pl.ds(here, channels), :] = masked[:, v * LANES : (v + 1) * LANES]
    for rows, stack, prod in sets:
        size = rows.shape[0] // 4
        planes = jnp.dot(rows[...], expand[...], preferred_element_type=jnp.float32).astype(jnp.bfloat16)
        for v in range(4):
            for a in range(2):
                at = slice((2 * v + a) * LANES, (2 * v + a + 1) * LANES)
                plane = planes[v * size : (v + 1) * size, a * LANES : (a + 1) * LANES]
                stack[0:size, at] = shifted(plane, 1)
                stack[size : 2 * size, at] = plane
                stack[2 * size : 3 * size, at] = shifted(plane, -1)
    for rows, stack, prod in sets:
        prod[...] = jnp.dot(wide[...], stack[...], preferred_element_type=jnp.float32)
    for rows, stack, prod in sets:
        results = []
        for layer in range(SIDE):
            sums = []
            for q in range(3):
                total = None
                for p in range(3):
                    inside = layer + p - 1
                    if 0 <= inside < SIDE:
                        first = (3 * p + q) * channels
                        part = prod[first : first + channels, inside * LANES : (inside + 1) * LANES]
                        total = part if total is None else total + part
                sums.append(total)
            results.append(sums[1] + shifted(sums[0], PAD) + shifted(sums[2], -PAD))
        yield results


def block_parts(group, step, me, live, occ, xs):
    n = len(xs)
    channels = xs[0].shape[1]
    blocks = []
    for b in range(group):
        row = active_row(occ, step * group + b, live).astype(jnp.bfloat16)
        blocks.append((row, [(mod(me ^ key, n) * channels, x[b]) for key, x in enumerate(xs)]))
    return blocks


def near_kernel(group, me_ref, live_ref, occ, weights, expand, *refs):
    n = len(refs) - 2 - 3 * group
    xs = refs[:n]
    out, wide = refs[n : n + 2]
    channels = weights.shape[1]
    step = pl.program_id(0)
    me = me_ref[0]

    @pl.when(step == 0)
    def _():
        half_weights(weights, wide, div(me, n) == 1)

    blocks = block_parts(group, step, me, live_ref[0], occ, xs)
    sets = [refs[n + 2 + 3 * b : n + 5 + 3 * b] for b in range(group)]
    for b, results in enumerate(conv_blocks(blocks, sets, wide, expand)):
        for layer, result in enumerate(results):
            out[step * group + b, :, layer * LANES : (layer + 1) * LANES] = result


def far_kernel(group, me_ref, live_ref, occ, weights, expand, gather, near, *refs):
    n = len(refs) - 5 - 3 * group
    xs = refs[:n]
    out, rim, shell = refs[n : n + 3]
    wide, packed = refs[n + 3 : n + 5]
    channels = weights.shape[1]
    step = pl.program_id(0)
    me = me_ref[0]

    @pl.when(step == 0)
    def _():
        half_weights(weights, wide, div(me, n) == 0)

    blocks = block_parts(group, step, me, live_ref[0], occ, xs)
    sets = [refs[n + 5 + 3 * b : n + 8 + 3 * b] for b in range(group)]
    for b, results in enumerate(conv_blocks(blocks, sets, wide, expand)):
        for layer, result in enumerate(results):
            at = slice(layer * LANES, (layer + 1) * LANES)
            total = result + near[step * group + b, :, at]
            out[b, :, at] = total
            if 0 < layer < SIDE - 1:
                packed[b, :, (layer - 1) * LANES : layer * LANES] = total.astype(jnp.bfloat16)
            else:
                side = slice(LANES * (layer > 0), LANES * (layer > 0) + LANES)
                rim[step * group + b, :, side] = total
    picked = jnp.dot(
        packed[...].reshape(group * channels, (SIDE - 2) * LANES),
        gather[LANES : (SIDE - 1) * LANES, :],
        preferred_element_type=jnp.float32,
    )
    shell[pl.ds(step * group, group)] = picked.astype(jnp.bfloat16).reshape(packed.shape[:2] + shell.shape[2:])


def edge_mask(lane, quarter, e):
    return jnp.logical_and((lane >> 5) == quarter, ((lane >> 3) & 3) == e)


def halo_kernel(slots, cap, me_ref, send, weights, expand, gather, shell, base, *refs):
    n = len(refs) - 8
    hs = refs[:n]
    added, faces = refs[n : n + 2]
    wide, rows, stack, prod, packed, edges = refs[n + 2 :]
    channels, every = weights.shape[1:]
    me = me_ref[0]
    for side in range(2):
        for g in range(3):
            for r in range(3):
                wide[side, g * channels : (g + 1) * channels, r * every : (r + 1) * every] = weights[
                    18 * side + 3 * g + r
                ]
    for r in range(slots):
        for key, h in enumerate(hs):
            at = pl.multiple_of((me ^ key) * channels + r * every, channels)
            rows[pl.ds(at, channels), :] = h[r]
    for r in range(slots):
        planes = jnp.dot(
            rows[r * every : (r + 1) * every, :], expand[...], preferred_element_type=jnp.float32
        ).astype(jnp.bfloat16)
        at = slice(r * LANES, (r + 1) * LANES)
        for side in range(2):
            plane = planes[:, (1 - side) * LANES : (2 - side) * LANES]
            stack[side, 0:every, at] = shifted(plane, 1)
            stack[side, every : 2 * every, at] = plane
            stack[side, 2 * every : 3 * every, at] = shifted(plane, -1)
    for side in range(2):
        prod[side] = jnp.dot(wide[side], stack[side], preferred_element_type=jnp.float32)
    for r in range(slots):
        at = slice(r * LANES, (r + 1) * LANES)
        for side in range(2):
            sums = [prod[side, q * channels : (q + 1) * channels, at] for q in range(3)]
            result = sums[1] + shifted(sums[0], PAD) + shifted(sums[2], -PAD)
            here = slice(side * LANES, (side + 1) * LANES)
            added[r, :, here] = result
            packed[r, :, here] = (base[r, :, here] + result).astype(jnp.bfloat16)
    picked = jnp.dot(packed[...].reshape(slots * channels, 2 * LANES), gather[...], preferred_element_type=jnp.float32)
    lane = lax.broadcasted_iota(jnp.int32, (channels, LANES), 1)
    for s in range(slots):
        mine = picked[s * channels : (s + 1) * channels].astype(jnp.bfloat16) + shell[s]
        for d in range(2):
            pair = mine[:, d * LANES : (d + 1) * LANES]
            faces[send[(2 * d + 1) * slots + s], :, :HALF] = pair[:, :HALF]
            faces[send[2 * d * slots + s], :, HALF:] = pair[:, HALF:]
        edge = mine[:, 2 * LANES :].astype(jnp.float32)
        for e in range(4):
            slot = send[(4 + e) * slots + s]
            pltpu.store(edges.at[slot >> 2], edge, mask=edge_mask(lane, slot & 3, e))
    quarter = slots // 4
    for peer in range(edges.shape[0] // quarter):
        at = peer * (2 * cap + quarter) + 2 * cap
        faces[at : at + quarter] = edges[peer * quarter : (peer + 1) * quarter].astype(jnp.bfloat16)


def squeeze_kernel(part, bias, squeeze, base, added, out):
    for n in range(part):
        b = pl.program_id(0) * part + n
        for v in range(4):
            pair = base[n, :, 2 * v * LANES : 2 * (v + 1) * LANES] + bias[...]
            if v in (0, 3):
                extra = added[b, :, LANES * (v > 0) : LANES * (v > 0) + LANES]
                zero = jnp.zeros_like(extra)
                pair = pair + jnp.concatenate([extra, zero] if v == 0 else [zero, extra], axis=1)
            total = None
            for _ in range(3):
                term = pair.astype(jnp.bfloat16)
                pair = pair - term.astype(jnp.float32)
                flat = jnp.dot(term, squeeze[...], preferred_element_type=jnp.float32)
                total = flat if total is None else total + flat
            out[b, :, v * LANES : (v + 1) * LANES] = total


def finish_kernel(slots, recv, live_ref, occ, scatter, base, faces, out, shell):
    channels = base.shape[1]
    live = live_ref[0]
    lane = lax.broadcasted_iota(jnp.int32, (channels, LANES), 1)
    for r in range(slots):
        for d in range(2):
            up = faces[recv[2 * d * slots + r]]
            down = faces[recv[(2 * d + 1) * slots + r]]
            shell[r, :, d * LANES : (d + 1) * LANES] = jnp.where(lane < HALF, down, up)
        total = jnp.zeros((channels, LANES), jnp.bfloat16)
        for e in range(4):
            slot = recv[(4 + e) * slots + r]
            total = jnp.where(edge_mask(lane, slot & 3, e), faces[slot >> 2], total)
        shell[r, :, 2 * LANES :] = total
    added = jnp.dot(
        shell[...].reshape(slots * channels, 3 * LANES), scatter[...], preferred_element_type=jnp.float32
    )
    for r in range(slots):
        summed = base[r] + added[r * channels : (r + 1) * channels]
        out[r] = (summed * active_row(occ, r, live)).astype(jnp.bfloat16)


def spread(x, axis, near, size):
    have = {0: x}
    bit = near >> 1
    while bit:
        for key in list(have):
            have[key ^ bit] = lax.ppermute(have[key], axis, [(n, n ^ bit) for n in range(size)])
        bit >>= 1
    return [have[key] for key in range(near)]


def spread_direct(x, axis, size):
    return [x] + [lax.ppermute(x, axis, [(n, n ^ key) for n in range(size)]) for key in range(1, size)]


def shards(features, weights, bias, occupancy, live, neighbours):
    slots, channels, voxels = features.shape
    peers = lax.axis_size("blk")
    members = lax.axis_size("ch")
    cap = max(2, 2 * slots // peers)
    every = channels * members
    group = 8 if slots % 8 == 0 else slots
    part = 4
    bf16, f32, i32 = jnp.bfloat16, jnp.float32, jnp.int32
    smem = pl.BlockSpec(memory_space=pltpu.SMEM)
    vmem = pl.BlockSpec(memory_space=pltpu.VMEM)
    resident = lambda x: pltpu.with_memory_space_constraint(x, pltpu.VMEM)
    params = pltpu.CompilerParams(vmem_limit_bytes=VMEM_LIMIT)
    expand, gather, scatter = (jnp.asarray(t, bf16) for t in tables())
    squeeze = jnp.asarray(tables()[0].T, bf16)
    outermost = jnp.asarray(np.concatenate([tables()[1][:LANES], tables()[1][-LANES:]]), bf16)
    place = lax.axis_index("blk").astype(i32).reshape(1)
    member = lax.axis_index("ch").astype(i32).reshape(1)
    nbr = neighbours.transpose(1, 2, 0)

    def table(kinds, name, nbr):
        return pl.pallas_call(
            functools.partial(table_kernel, kinds, peers, cap, slots),
            out_shape=jax.ShapeDtypeStruct((len(kinds) * slots,), i32),
            in_specs=[smem, smem],
            out_specs=smem,
            scratch_shapes=[pltpu.SMEM((len(kinds) * peers,), i32)],
            name=name,
        )(place, nbr)

    corner = pl.BlockSpec((slots, channels, LANES), lambda n: (0, 0, 0))
    corner_last = pl.BlockSpec((slots, channels, LANES), lambda n: (0, 0, voxels // LANES - 1))
    outgoing = pl.pallas_call(
        functools.partial(pack_kernel, peers, cap, slots),
        grid=(1,),
        out_shape=jax.ShapeDtypeStruct((peers * cap, channels, LANES), bf16),
        in_specs=[smem, smem, smem, vmem, corner, corner_last],
        out_specs=vmem,
        scratch_shapes=[pltpu.SMEM((2 * peers,), i32)],
        compiler_params=params,
        name="pack_layers",
    )(place, live, nbr, occupancy, features, features)
    outgoing, shipped = lax.optimization_barrier((outgoing, features))
    half = members // 2
    across = lax.ppermute(shipped, "ch", [(n, n ^ half) for n in range(members)])
    beside = spread(shipped, "ch", half, members)
    arrived = lax.all_to_all(outgoing, "blk", split_axis=0, concat_axis=0, tiled=True)

    per_block = lambda width: pl.BlockSpec((group, channels, width), lambda n: (n, 0, 0))
    some = lambda width: pl.BlockSpec((part, channels, width), lambda n: (n, 0, 0))
    buffers = [
        pltpu.VMEM((4 * half * channels, LANES), bf16),
        pltpu.VMEM((3 * half * channels, SIDE * LANES), bf16),
        pltpu.VMEM((9 * channels, SIDE * LANES), f32),
    ] * group
    wide = pltpu.VMEM((9 * channels, 3 * half * channels), bf16)
    near = pl.pallas_call(
        functools.partial(near_kernel, group),
        grid=(slots // group,),
        out_shape=pltpu.VMEM((slots, channels, SIDE * LANES), f32),
        in_specs=[smem, smem, vmem, vmem, vmem] + [per_block(voxels)] * half,
        out_specs=vmem,
        scratch_shapes=[wide] + buffers,
        compiler_params=params,
        name="convolve_near",
    )(member, live, occupancy, weights, expand, *beside)
    near, later = lax.optimization_barrier((near, nbr))
    across, near = lax.optimization_barrier((across, near))
    remote = spread(across, "ch", half, members)

    send, incoming = pl.pallas_call(
        functools.partial(early_kernel, peers, cap, slots),
        out_shape=(jax.ShapeDtypeStruct((8 * slots,), i32), jax.ShapeDtypeStruct((2 * slots,), i32)),
        in_specs=[smem, smem],
        out_specs=(smem, smem),
        scratch_shapes=[pltpu.SMEM((8 * peers,), i32), pltpu.SMEM((2 * peers,), i32)],
        name="early_tables",
    )(place, later)
    arrived, incoming = lax.optimization_barrier((arrived, incoming))
    layers = pl.pallas_call(
        functools.partial(order_kernel, slots),
        out_shape=pltpu.VMEM((slots, channels, LANES), bf16),
        in_specs=[smem, vmem],
        out_specs=vmem,
        compiler_params=params,
        name="order_layers",
    )(incoming, resident(arrived))
    halo = spread_direct(layers, "ch", members)

    *remote, _ = lax.optimization_barrier((*remote, layers))
    base, rim, shell = pl.pallas_call(
        functools.partial(far_kernel, group),
        grid=(slots // group,),
        out_shape=(
            jax.ShapeDtypeStruct((slots, channels, SIDE * LANES), f32),
            pltpu.VMEM((slots, channels, 2 * LANES), f32),
            pltpu.VMEM((slots, channels, 3 * LANES), bf16),
        ),
        in_specs=[smem, smem, vmem, vmem, vmem, vmem, vmem] + [per_block(voxels)] * half,
        out_specs=(per_block(SIDE * LANES), vmem, vmem),
        scratch_shapes=[wide, pltpu.VMEM((group, channels, (SIDE - 2) * LANES), bf16)] + buffers,
        compiler_params=params,
        name="convolve_far",
    )(member, live, occupancy, weights, expand, gather, resident(near), *[resident(x) for x in remote])

    added, faces = pl.pallas_call(
        functools.partial(halo_kernel, slots, cap),
        out_shape=(
            pltpu.VMEM((slots, channels, 2 * LANES), f32),
            pltpu.VMEM((peers * (2 * cap + slots // 4), channels, LANES), bf16),
        ),
        in_specs=[smem, smem, vmem, vmem, vmem, vmem, vmem] + [vmem] * members,
        out_specs=(vmem, vmem),
        scratch_shapes=[
            pltpu.VMEM((2, 3 * channels, 3 * every), bf16),
            pltpu.VMEM((slots * every, LANES), bf16),
            pltpu.VMEM((2, 3 * every, slots * LANES), bf16),
            pltpu.VMEM((2, 3 * channels, slots * LANES), f32),
            pltpu.VMEM((slots, channels, 2 * LANES), bf16),
            pltpu.VMEM((peers * slots // 4, channels, LANES), f32),
        ],
        compiler_params=params,
        name="convolve_halo",
    )(
        member, send, weights, expand, outermost, resident(shell), resident(rim),
        *[resident(x) for x in halo],
    )

    faces = lax.all_to_all(faces, "blk", split_axis=0, concat_axis=0, tiled=True)

    base = pl.pallas_call(
        functools.partial(squeeze_kernel, part),
        grid=(slots // part,),
        out_shape=pltpu.VMEM((slots, channels, voxels), f32),
        in_specs=[vmem, vmem, some(SIDE * LANES), vmem],
        out_specs=vmem,
        compiler_params=params,
        name="squeeze_planes",
    )(bias[:, None], squeeze, base, resident(added))

    return pl.pallas_call(
        functools.partial(finish_kernel, slots),
        out_shape=jax.ShapeDtypeStruct((slots, channels, voxels), bf16),
        in_specs=[smem, smem] + [vmem] * 4,
        out_specs=vmem,
        scratch_shapes=[pltpu.VMEM((slots, channels, 3 * LANES), bf16)],
        compiler_params=params,
        name="finish",
    )(
        table(tuple(range(8)), "slot_table", nbr), live, occupancy, scatter, resident(base),
        resident(faces),
    )


def solution(mesh):
    in_specs = (P("blk", "ch", None), P(None, "ch", None), P("ch"), P("blk", None), P("blk"), P())
    out_specs = P("blk", "ch", None)
    return jax.shard_map(shards, mesh=mesh, in_specs=in_specs, out_specs=out_specs, check_vma=False)
```

```python
import functools

import jax
import jax.numpy as jnp
import numpy as np
from jax import lax
from jax.experimental import pallas as pl
from jax.experimental.pallas import tpu as pltpu
from jax.sharding import PartitionSpec as P

SIDE = 8
PAD = SIDE + 2
LANES = 128
HALF = SIDE * SIDE
VMEM_LIMIT = 57 * 1024 * 1024

FACES = [(1, 0), (1, 1), (2, 0), (2, 1)]
EDGES = [(0, 0), (0, 1), (1, 0), (1, 1)]


def outer(q):
    return PAD - 1 if q == 0 else 0


def inner(q):
    return 0 if q == 0 else SIDE - 1


@functools.lru_cache(None)
def tables():
    expand = np.zeros((LANES, 2 * LANES), np.float32)
    for a in range(2):
        for j in range(SIDE):
            for k in range(SIDE):
                expand[a * HALF + j * SIDE + k, a * LANES + (j + 1) * PAD + k + 1] = 1
    gather = np.zeros((SIDE * LANES, 3 * LANES), np.float32)
    scatter = np.zeros((3 * LANES, SIDE * HALF), np.float32)
    for i in range(SIDE):
        for d, q in FACES:
            for a in range(SIDE):
                lane = (d - 1) * LANES + (1 - q) * HALF + i * SIDE + a
                if d == 1:
                    source, target = outer(q) * PAD + a + 1, inner(q) * SIDE + a
                else:
                    source, target = (a + 1) * PAD + outer(q), a * SIDE + inner(q)
                gather[i * LANES + source, lane] = 1
                scatter[lane, i * HALF + target] = 1
        for quarter in range(4):
            for e, (qj, qk) in enumerate(EDGES):
                lane = 2 * LANES + quarter * 4 * SIDE + e * SIDE + i
                gather[i * LANES + outer(qj) * PAD + outer(qk), lane] = 1
                scatter[lane, i * HALF + inner(qj) * SIDE + inner(qk)] = 1
    return expand, gather, scatter


def div(value, size):
    return value >> (size.bit_length() - 1) if size & (size - 1) == 0 else lax.div(value, size)


def mod(value, size):
    return value & (size - 1) if size & (size - 1) == 0 else lax.rem(value, size)


def popcount(x):
    x = x - ((x >> 1) & 0x55555555)
    x = (x & 0x33333333) + ((x >> 2) & 0x33333333)
    x = (x + (x >> 4)) & 0x0F0F0F0F
    x = x + (x >> 8)
    return (x + (x >> 16)) & 0x3F


def each(size, step, unrolled):
    if unrolled:
        for n in range(size):
            step(n, 0)
    else:
        lax.fori_loop(0, size, step, 0)


def clear(ref, size, unrolled=False):
    def step(n, _):
        ref[n] = 0
        return 0

    each(size, step, unrolled)


def slot_of(kind, peer, place, cap, slots):
    if kind < 4:
        return peer * (2 * cap + slots // 4) + (FACES[kind][0] - 1) * cap + place
    return peer * cap + place


def neighbour(nbr, b, d, q):
    return nbr[d, q, b]


def dest(nbr, b, kind):
    return neighbour(nbr, b, *FACES[kind])


def source(nbr, r, kind):
    if kind >= 8:
        return neighbour(nbr, r, 0, 1 - (kind - 8))
    if kind < 4:
        d, q = FACES[kind]
        return neighbour(nbr, r, d, 1 - q)
    qj, qk = EDGES[kind - 4]
    return neighbour(nbr, neighbour(nbr, r, 2, 1 - qk), 1, 1 - qj)


def send_slots(peers, cap, slots, me_ref, nbr, send, count, unrolled):
    first = me_ref[0] * slots
    clear(count, 4 * peers, unrolled)

    def place_of(s, _):
        for kind in range(4):
            peer = div(dest(nbr, first + s, kind), slots)
            place = count[kind * peers + peer]
            count[kind * peers + peer] = place + 1
            send[kind * slots + s] = slot_of(kind, peer, place, cap, slots)
        return 0

    each(slots, place_of, unrolled)


def arrival_slots(kinds, peers, cap, slots, me_ref, nbr, recv, mask, unrolled=False):
    first = me_ref[0] * slots
    clear(mask, len(kinds) * peers, unrolled)

    def gather(s, _):
        for n, kind in enumerate(kinds):
            b = source(nbr, first + s, kind)
            at = n * peers + div(b, slots)
            mask[at] = mask[at] | (1 << mod(b, slots))
        return 0

    each(slots, gather, unrolled)

    def rank(r, _):
        for n, kind in enumerate(kinds):
            b = source(nbr, first + r, kind)
            peer = div(b, slots)
            before = popcount(mask[n * peers + peer] & ((1 << mod(b, slots)) - 1))
            recv[n * slots + r] = slot_of(kind, peer, before, cap, slots)
        return 0

    each(slots, rank, unrolled)


def late_kernel(peers, cap, slots, me_ref, nbr, recv, mask):
    arrival_slots(range(4), peers, cap, slots, me_ref, nbr, recv, mask)
    me = me_ref[0]

    def place_of(r, _):
        for kind in range(4, 8):
            b = source(nbr, me * slots + r, kind)
            row = div(b, slots) * (2 * cap + slots // 4) + 2 * cap
            recv[kind * slots + r] = row * 4 + mod(b, slots)
        return 0

    lax.fori_loop(0, slots, place_of, 0)


def active_row(occ_ref, s, live):
    return occ_ref[pl.ds(s, 1), :].astype(jnp.float32) * (s < live).astype(jnp.float32)


def pack_kernel(peers, cap, slots, me_ref, live_ref, nbr, occ, low, high, out, count):
    first = me_ref[0] * slots
    live = live_ref[0]
    clear(count, 2 * peers)
    for s in range(slots):
        row = active_row(occ, s, live).astype(jnp.bfloat16)
        for q in range(2):
            peer = div(neighbour(nbr, first + s, 0, q), slots)
            place = count[q * peers + peer]
            count[q * peers + peer] = place + 1
            half = slice(0, HALF) if q == 1 else slice(HALF, LANES)
            face = low if q == 1 else high
            lanes = row[:, :LANES] if q == 1 else row[:, -LANES:]
            out[peer * cap + place, :, half] = (face[s] * lanes)[:, half]


def order_kernel(slots, recv, arrived, out):
    lane = lax.broadcasted_iota(jnp.int32, arrived.shape[1:], 1)
    for r in range(slots):
        up = arrived[recv[r]]
        down = arrived[recv[slots + r]]
        out[r] = jnp.where(lane < HALF, down, up)


def shifted(plane, by):
    return pltpu.roll(plane, by % LANES, axis=1)


def half_weights(weights, wide, upper):
    channels, every = weights.shape[1:]
    half = every // 2
    for g in range(9):
        for r in range(3):
            w = weights[3 * g + r]
            wide[g * channels : (g + 1) * channels, r * half : (r + 1) * half] = jnp.where(
                upper, w[:, half:], w[:, :half]
            )


def conv_blocks(blocks, sets, wide, expand):
    channels = wide.shape[0] // 9
    for (row, parts), (rows, stack, prod) in zip(blocks, sets):
        size = rows.shape[0] // 4
        for at, x in parts:
            masked = x * row
            for v in range(4):
                here = pl.multiple_of(v * size + at, channels)
                rows[pl.ds(here, channels), :] = masked[:, v * LANES : (v + 1) * LANES]
    for rows, stack, prod in sets:
        size = rows.shape[0] // 4
        planes = jnp.dot(rows[...], expand[...], preferred_element_type=jnp.float32).astype(jnp.bfloat16)
        for v in range(4):
            for a in range(2):
                at = slice((2 * v + a) * LANES, (2 * v + a + 1) * LANES)
                plane = planes[v * size : (v + 1) * size, a * LANES : (a + 1) * LANES]
                stack[0:size, at] = shifted(plane, 1)
                stack[size : 2 * size, at] = plane
                stack[2 * size : 3 * size, at] = shifted(plane, -1)
    for rows, stack, prod in sets:
        prod[...] = jnp.dot(wide[...], stack[...], preferred_element_type=jnp.float32)
    for rows, stack, prod in sets:
        results = []
        for layer in range(SIDE):
            sums = []
            for q in range(3):
                total = None
                for p in range(3):
                    inside = layer + p - 1
                    if 0 <= inside < SIDE:
                        first = (3 * p + q) * channels
                        part = prod[first : first + channels, inside * LANES : (inside + 1) * LANES]
                        total = part if total is None else total + part
                sums.append(total)
            results.append(sums[1] + shifted(sums[0], PAD) + shifted(sums[2], -PAD))
        yield results


def block_parts(group, step, me, live, occ, xs):
    n = len(xs)
    channels = xs[0].shape[1]
    blocks = []
    for b in range(group):
        row = active_row(occ, step * group + b, live).astype(jnp.bfloat16)
        blocks.append((row, [(mod(me ^ key, n) * channels, x[b]) for key, x in enumerate(xs)]))
    return blocks


def near_kernel(peers, cap, group, place_ref, me_ref, live_ref, nbr, occ, weights, expand, *refs):
    n = len(refs) - 6 - 3 * group
    xs = refs[:n]
    out, send, recv, wide, count, mask = refs[n : n + 6]
    sets = [refs[n + 6 + 3 * b : n + 9 + 3 * b] for b in range(group)]
    me = me_ref[0]
    send_slots(peers, cap, group, place_ref, nbr, send, count, True)
    arrival_slots((8, 9), peers, cap, group, place_ref, nbr, recv, mask, True)
    half_weights(weights, wide, div(me, n) == 1)
    blocks = block_parts(group, 0, me, live_ref[0], occ, xs)
    for b, results in enumerate(conv_blocks(blocks, sets, wide, expand)):
        for layer, result in enumerate(results):
            out[b, :, layer * LANES : (layer + 1) * LANES] = result


def far_kernel(group, me_ref, live_ref, occ, weights, expand, gather, near, *refs):
    n = len(refs) - 5 - 3 * group
    xs = refs[:n]
    out, rim, shell = refs[n : n + 3]
    wide, packed = refs[n + 3 : n + 5]
    channels = weights.shape[1]
    step = pl.program_id(0)
    me = me_ref[0]

    @pl.when(step == 0)
    def _():
        half_weights(weights, wide, div(me, n) == 0)

    blocks = block_parts(group, step, me, live_ref[0], occ, xs)
    sets = [refs[n + 5 + 3 * b : n + 8 + 3 * b] for b in range(group)]
    for b, results in enumerate(conv_blocks(blocks, sets, wide, expand)):
        for layer, result in enumerate(results):
            at = slice(layer * LANES, (layer + 1) * LANES)
            total = result + near[step * group + b, :, at]
            out[b, :, at] = total
            if 0 < layer < SIDE - 1:
                packed[b, :, (layer - 1) * LANES : layer * LANES] = total.astype(jnp.bfloat16)
            else:
                side = slice(LANES * (layer > 0), LANES * (layer > 0) + LANES)
                rim[step * group + b, :, side] = total
    picked = jnp.dot(
        packed[...].reshape(group * channels, (SIDE - 2) * LANES),
        gather[LANES : (SIDE - 1) * LANES, :],
        preferred_element_type=jnp.float32,
    )
    shell[pl.ds(step * group, group)] = picked.astype(jnp.bfloat16).reshape(packed.shape[:2] + shell.shape[2:])


def edge_mask(lane, quarter, e):
    return jnp.logical_and((lane >> 5) == quarter, ((lane >> 3) & 3) == e)


def halo_kernel(slots, cap, me_ref, send, weights, expand, gather, shell, base, *refs):
    n = len(refs) - 8
    hs = refs[:n]
    added, faces = refs[n : n + 2]
    wide, rows, stack, prod, packed, edges = refs[n + 2 :]
    channels, every = weights.shape[1:]
    me = me_ref[0]
    for side in range(2):
        for g in range(3):
            for r in range(3):
                wide[side, g * channels : (g + 1) * channels, r * every : (r + 1) * every] = weights[
                    18 * side + 3 * g + r
                ]
    for r in range(slots):
        for key, h in enumerate(hs):
            at = pl.multiple_of((me ^ key) * channels + r * every, channels)
            rows[pl.ds(at, channels), :] = h[r]
    for r in range(slots):
        planes = jnp.dot(
            rows[r * every : (r + 1) * every, :], expand[...], preferred_element_type=jnp.float32
        ).astype(jnp.bfloat16)
        at = slice(r * LANES, (r + 1) * LANES)
        for side in range(2):
            plane = planes[:, (1 - side) * LANES : (2 - side) * LANES]
            stack[side, 0:every, at] = shifted(plane, 1)
            stack[side, every : 2 * every, at] = plane
            stack[side, 2 * every : 3 * every, at] = shifted(plane, -1)
    for side in range(2):
        prod[side] = jnp.dot(wide[side], stack[side], preferred_element_type=jnp.float32)
    for r in range(slots):
        at = slice(r * LANES, (r + 1) * LANES)
        for side in range(2):
            sums = [prod[side, q * channels : (q + 1) * channels, at] for q in range(3)]
            result = sums[1] + shifted(sums[0], PAD) + shifted(sums[2], -PAD)
            here = slice(side * LANES, (side + 1) * LANES)
            added[r, :, here] = result
            packed[r, :, here] = (base[r, :, here] + result).astype(jnp.bfloat16)
    picked = jnp.dot(packed[...].reshape(slots * channels, 2 * LANES), gather[...], preferred_element_type=jnp.float32)
    for s in range(slots):
        mine = picked[s * channels : (s + 1) * channels].astype(jnp.bfloat16) + shell[s]
        for d in range(2):
            pair = mine[:, d * LANES : (d + 1) * LANES]
            faces[send[(2 * d + 1) * slots + s], :, :HALF] = pair[:, :HALF]
            faces[send[2 * d * slots + s], :, HALF:] = pair[:, HALF:]
        quarter = slice((s & 3) * 4 * SIDE, ((s & 3) + 1) * 4 * SIDE)
        edges[s >> 2, :, quarter] = mine[:, 2 * LANES :][:, quarter]
    size = 2 * cap + slots // 4
    for peer in range(faces.shape[0] // size):
        faces[peer * size + 2 * cap : (peer + 1) * size] = edges[...]


def squeeze_kernel(part, bias, squeeze, base, added, out):
    for n in range(part):
        b = pl.program_id(0) * part + n
        for v in range(4):
            pair = base[n, :, 2 * v * LANES : 2 * (v + 1) * LANES] + bias[...]
            if v in (0, 3):
                extra = added[b, :, LANES * (v > 0) : LANES * (v > 0) + LANES]
                zero = jnp.zeros_like(extra)
                pair = pair + jnp.concatenate([extra, zero] if v == 0 else [zero, extra], axis=1)
            total = None
            for _ in range(3):
                term = pair.astype(jnp.bfloat16)
                pair = pair - term.astype(jnp.float32)
                flat = jnp.dot(term, squeeze[...], preferred_element_type=jnp.float32)
                total = flat if total is None else total + flat
            out[b, :, v * LANES : (v + 1) * LANES] = total


def finish_kernel(slots, recv, live_ref, occ, scatter, base, faces, out, shell):
    channels = base.shape[1]
    live = live_ref[0]
    lane = lax.broadcasted_iota(jnp.int32, (channels, LANES), 1)
    for r in range(slots):
        for d in range(2):
            up = faces[recv[2 * d * slots + r]]
            down = faces[recv[(2 * d + 1) * slots + r]]
            shell[r, :, d * LANES : (d + 1) * LANES] = jnp.where(lane < HALF, down, up)
        total = jnp.zeros((channels, LANES), jnp.bfloat16)
        for e in range(4):
            slot = recv[(4 + e) * slots + r]
            total = jnp.where(edge_mask(lane, slot & 3, e), faces[slot >> 2], total)
        shell[r, :, 2 * LANES :] = total
    added = jnp.dot(
        shell[...].reshape(slots * channels, 3 * LANES), scatter[...], preferred_element_type=jnp.float32
    )
    for r in range(slots):
        summed = base[r] + added[r * channels : (r + 1) * channels]
        out[r] = (summed * active_row(occ, r, live)).astype(jnp.bfloat16)


def spread(x, axis, near, size):
    have = {0: x}
    bit = near >> 1
    while bit:
        for key in list(have):
            have[key ^ bit] = lax.ppermute(have[key], axis, [(n, n ^ bit) for n in range(size)])
        bit >>= 1
    return [have[key] for key in range(near)]


def spread_direct(x, axis, size):
    return [x] + [lax.ppermute(x, axis, [(n, n ^ key) for n in range(size)]) for key in range(1, size)]


def shards(features, weights, bias, occupancy, live, neighbours):
    slots, channels, voxels = features.shape
    peers = lax.axis_size("blk")
    members = lax.axis_size("ch")
    cap = max(2, 2 * slots // peers)
    every = channels * members
    group = 8 if slots % 8 == 0 else slots
    part = 4
    bf16, f32, i32 = jnp.bfloat16, jnp.float32, jnp.int32
    smem = pl.BlockSpec(memory_space=pltpu.SMEM)
    vmem = pl.BlockSpec(memory_space=pltpu.VMEM)
    resident = lambda x: pltpu.with_memory_space_constraint(x, pltpu.VMEM)
    params = pltpu.CompilerParams(vmem_limit_bytes=VMEM_LIMIT)
    expand, gather, scatter = (jnp.asarray(t, bf16) for t in tables())
    squeeze = jnp.asarray(tables()[0].T, bf16)
    outermost = jnp.asarray(np.concatenate([tables()[1][:LANES], tables()[1][-LANES:]]), bf16)
    place = lax.axis_index("blk").astype(i32).reshape(1)
    member = lax.axis_index("ch").astype(i32).reshape(1)
    nbr = neighbours.transpose(1, 2, 0)

    corner = pl.BlockSpec((slots, channels, LANES), lambda n: (0, 0, 0))
    corner_last = pl.BlockSpec((slots, channels, LANES), lambda n: (0, 0, voxels // LANES - 1))
    outgoing = pl.pallas_call(
        functools.partial(pack_kernel, peers, cap, slots),
        grid=(1,),
        out_shape=jax.ShapeDtypeStruct((peers * cap, channels, LANES), bf16),
        in_specs=[smem, smem, smem, vmem, corner, corner_last],
        out_specs=vmem,
        scratch_shapes=[pltpu.SMEM((2 * peers,), i32)],
        compiler_params=params,
        name="pack_layers",
    )(place, live, nbr, occupancy, features, features)
    outgoing, shipped = lax.optimization_barrier((outgoing, features))
    half = members // 2
    across = lax.ppermute(shipped, "ch", [(n, n ^ half) for n in range(members)])
    arrived = lax.all_to_all(outgoing, "blk", split_axis=0, concat_axis=0, tiled=True)
    beside = spread(shipped, "ch", half, members)

    per_block = lambda width: pl.BlockSpec((group, channels, width), lambda n: (n, 0, 0))
    some = lambda width: pl.BlockSpec((part, channels, width), lambda n: (n, 0, 0))
    buffers = lambda count: [
        pltpu.VMEM((4 * half * channels, LANES), bf16),
        pltpu.VMEM((3 * half * channels, SIDE * LANES), bf16),
        pltpu.VMEM((9 * channels, SIDE * LANES), f32),
    ] * count
    wide = pltpu.VMEM((9 * channels, 3 * half * channels), bf16)
    near, send, incoming = pl.pallas_call(
        functools.partial(near_kernel, peers, cap, slots),
        out_shape=(
            pltpu.VMEM((slots, channels, SIDE * LANES), f32),
            jax.ShapeDtypeStruct((4 * slots,), i32),
            jax.ShapeDtypeStruct((2 * slots,), i32),
        ),
        in_specs=[smem, smem, smem, smem, vmem, vmem, vmem] + [vmem] * half,
        out_specs=(vmem, smem, smem),
        scratch_shapes=[wide, pltpu.SMEM((4 * peers,), i32), pltpu.SMEM((2 * peers,), i32)] + buffers(slots),
        compiler_params=params,
        name="convolve_near",
    )(place, member, live, nbr, occupancy, weights, expand, *beside)
    across, near = lax.optimization_barrier((across, near))
    remote = spread(across, "ch", half, members)

    arrived, incoming = lax.optimization_barrier((arrived, incoming))
    layers = pl.pallas_call(
        functools.partial(order_kernel, slots),
        out_shape=pltpu.VMEM((slots, channels, LANES), bf16),
        in_specs=[smem, vmem],
        out_specs=vmem,
        compiler_params=params,
        name="order_layers",
    )(incoming, resident(arrived))
    halo = spread_direct(layers, "ch", members)

    *remote, _ = lax.optimization_barrier((*remote, layers))
    base, rim, shell = pl.pallas_call(
        functools.partial(far_kernel, group),
        grid=(slots // group,),
        out_shape=(
            jax.ShapeDtypeStruct((slots, channels, SIDE * LANES), f32),
            pltpu.VMEM((slots, channels, 2 * LANES), f32),
            pltpu.VMEM((slots, channels, 3 * LANES), bf16),
        ),
        in_specs=[smem, smem, vmem, vmem, vmem, vmem, vmem] + [per_block(voxels)] * half,
        out_specs=(per_block(SIDE * LANES), vmem, vmem),
        scratch_shapes=[wide, pltpu.VMEM((group, channels, (SIDE - 2) * LANES), bf16)] + buffers(group),
        compiler_params=params,
        name="convolve_far",
    )(member, live, occupancy, weights, expand, gather, resident(near), *[resident(x) for x in remote])

    added, faces = pl.pallas_call(
        functools.partial(halo_kernel, slots, cap),
        out_shape=(
            pltpu.VMEM((slots, channels, 2 * LANES), f32),
            pltpu.VMEM((peers * (2 * cap + slots // 4), channels, LANES), bf16),
        ),
        in_specs=[smem, smem, vmem, vmem, vmem, vmem, vmem] + [vmem] * members,
        out_specs=(vmem, vmem),
        scratch_shapes=[
            pltpu.VMEM((2, 3 * channels, 3 * every), bf16),
            pltpu.VMEM((slots * every, LANES), bf16),
            pltpu.VMEM((2, 3 * every, slots * LANES), bf16),
            pltpu.VMEM((2, 3 * channels, slots * LANES), f32),
            pltpu.VMEM((slots, channels, 2 * LANES), bf16),
            pltpu.VMEM((slots // 4, channels, LANES), bf16),
        ],
        compiler_params=params,
        name="convolve_halo",
    )(
        member, send, weights, expand, outermost, resident(shell), resident(rim),
        *[resident(x) for x in halo],
    )

    faces = lax.all_to_all(faces, "blk", split_axis=0, concat_axis=0, tiled=True)

    base = pl.pallas_call(
        functools.partial(squeeze_kernel, part),
        grid=(slots // part,),
        out_shape=pltpu.VMEM((slots, channels, voxels), f32),
        in_specs=[vmem, vmem, some(SIDE * LANES), vmem],
        out_specs=vmem,
        compiler_params=params,
        name="squeeze_planes",
    )(bias[:, None], squeeze, base, resident(added))

    recv = pl.pallas_call(
        functools.partial(late_kernel, peers, cap, slots),
        out_shape=jax.ShapeDtypeStruct((8 * slots,), i32),
        in_specs=[smem, smem],
        out_specs=smem,
        scratch_shapes=[pltpu.SMEM((4 * peers,), i32)],
        name="late_tables",
    )(place, nbr)
    return pl.pallas_call(
        functools.partial(finish_kernel, slots),
        out_shape=jax.ShapeDtypeStruct((slots, channels, voxels), bf16),
        in_specs=[smem, smem] + [vmem] * 4,
        out_specs=vmem,
        scratch_shapes=[pltpu.VMEM((slots, channels, 3 * LANES), bf16)],
        compiler_params=params,
        name="finish",
    )(
        recv, live, occupancy, scatter, resident(base), resident(faces),
    )


def solution(mesh):
    in_specs = (P("blk", "ch", None), P(None, "ch", None), P("ch"), P("blk", None), P("blk"), P())
    out_specs = P("blk", "ch", None)
    return jax.shard_map(shards, mesh=mesh, in_specs=in_specs, out_specs=out_specs, check_vma=False)
```

```python
import functools

import jax
import jax.numpy as jnp
import numpy as np
from jax import lax
from jax.experimental import pallas as pl
from jax.experimental.pallas import tpu as pltpu
from jax.sharding import PartitionSpec as P

SIDE = 8
PAD = SIDE + 2
LANES = 128
HALF = SIDE * SIDE
VMEM_LIMIT = 57 * 1024 * 1024

FACES = [(1, 0), (1, 1), (2, 0), (2, 1)]
EDGES = [(0, 0), (0, 1), (1, 0), (1, 1)]


def outer(q):
    return PAD - 1 if q == 0 else 0


def inner(q):
    return 0 if q == 0 else SIDE - 1


@functools.lru_cache(None)
def tables():
    expand = np.zeros((LANES, 2 * LANES), np.float32)
    for a in range(2):
        for j in range(SIDE):
            for k in range(SIDE):
                expand[a * HALF + j * SIDE + k, a * LANES + (j + 1) * PAD + k + 1] = 1
    gather = np.zeros((SIDE * LANES, 3 * LANES), np.float32)
    scatter = np.zeros((3 * LANES, SIDE * HALF), np.float32)
    for i in range(SIDE):
        for d, q in FACES:
            for a in range(SIDE):
                lane = (d - 1) * LANES + (1 - q) * HALF + i * SIDE + a
                if d == 1:
                    source, target = outer(q) * PAD + a + 1, inner(q) * SIDE + a
                else:
                    source, target = (a + 1) * PAD + outer(q), a * SIDE + inner(q)
                gather[i * LANES + source, lane] = 1
                scatter[lane, i * HALF + target] = 1
        for quarter in range(4):
            for e, (qj, qk) in enumerate(EDGES):
                lane = 2 * LANES + quarter * 4 * SIDE + e * SIDE + i
                gather[i * LANES + outer(qj) * PAD + outer(qk), lane] = 1
                scatter[lane, i * HALF + inner(qj) * SIDE + inner(qk)] = 1
    return expand, gather, scatter


def div(value, size):
    return value >> (size.bit_length() - 1) if size & (size - 1) == 0 else lax.div(value, size)


def mod(value, size):
    return value & (size - 1) if size & (size - 1) == 0 else lax.rem(value, size)


def popcount(x):
    x = x - ((x >> 1) & 0x55555555)
    x = (x & 0x33333333) + ((x >> 2) & 0x33333333)
    x = (x + (x >> 4)) & 0x0F0F0F0F
    x = x + (x >> 8)
    return (x + (x >> 16)) & 0x3F


def each(size, step, unrolled):
    if unrolled:
        for n in range(size):
            step(n, 0)
    else:
        lax.fori_loop(0, size, step, 0)


def clear(ref, size, unrolled=False):
    def step(n, _):
        ref[n] = 0
        return 0

    each(size, step, unrolled)


def slot_of(kind, peer, place, cap, slots):
    if kind < 4:
        return peer * (2 * cap + slots // 4) + (FACES[kind][0] - 1) * cap + place
    return peer * cap + place


def neighbour(nbr, b, d, q):
    return nbr[d, q, b]


def dest(nbr, b, kind):
    return neighbour(nbr, b, *FACES[kind])


def source(nbr, r, kind):
    if kind >= 8:
        return neighbour(nbr, r, 0, 1 - (kind - 8))
    if kind < 4:
        d, q = FACES[kind]
        return neighbour(nbr, r, d, 1 - q)
    qj, qk = EDGES[kind - 4]
    return neighbour(nbr, neighbour(nbr, r, 2, 1 - qk), 1, 1 - qj)


def send_slots(peers, cap, slots, me_ref, nbr, send, count, unrolled):
    first = me_ref[0] * slots
    clear(count, 4 * peers, unrolled)

    def place_of(s, _):
        for kind in range(4):
            peer = div(dest(nbr, first + s, kind), slots)
            place = count[kind * peers + peer]
            count[kind * peers + peer] = place + 1
            send[kind * slots + s] = slot_of(kind, peer, place, cap, slots)
        return 0

    each(slots, place_of, unrolled)


def arrival_slots(kinds, peers, cap, slots, me_ref, nbr, recv, mask, unrolled=False):
    first = me_ref[0] * slots
    clear(mask, len(kinds) * peers, unrolled)

    def gather(s, _):
        for n, kind in enumerate(kinds):
            b = source(nbr, first + s, kind)
            at = n * peers + div(b, slots)
            mask[at] = mask[at] | (1 << mod(b, slots))
        return 0

    each(slots, gather, unrolled)

    def rank(r, _):
        for n, kind in enumerate(kinds):
            b = source(nbr, first + r, kind)
            peer = div(b, slots)
            before = popcount(mask[n * peers + peer] & ((1 << mod(b, slots)) - 1))
            recv[n * slots + r] = slot_of(kind, peer, before, cap, slots)
        return 0

    each(slots, rank, unrolled)


def late_kernel(peers, cap, slots, me_ref, nbr, recv, mask):
    arrival_slots(range(4), peers, cap, slots, me_ref, nbr, recv, mask)
    me = me_ref[0]

    def place_of(r, _):
        for kind in range(4, 8):
            b = source(nbr, me * slots + r, kind)
            row = div(b, slots) * (2 * cap + slots // 4) + 2 * cap
            recv[kind * slots + r] = row * 4 + mod(b, slots)
        return 0

    lax.fori_loop(0, slots, place_of, 0)


def active_row(occ_ref, s, live):
    return occ_ref[pl.ds(s, 1), :].astype(jnp.float32) * (s < live).astype(jnp.float32)


def pack_kernel(peers, cap, slots, me_ref, live_ref, nbr, occ, low, high, out, count):
    first = me_ref[0] * slots
    live = live_ref[0]
    clear(count, 2 * peers)
    for s in range(slots):
        row = active_row(occ, s, live).astype(jnp.bfloat16)
        for q in range(2):
            peer = div(neighbour(nbr, first + s, 0, q), slots)
            place = count[q * peers + peer]
            count[q * peers + peer] = place + 1
            half = slice(0, HALF) if q == 1 else slice(HALF, LANES)
            face = low if q == 1 else high
            lanes = row[:, :LANES] if q == 1 else row[:, -LANES:]
            out[peer * cap + place, :, half] = (face[s] * lanes)[:, half]


def order_kernel(slots, recv, arrived, out):
    lane = lax.broadcasted_iota(jnp.int32, arrived.shape[1:], 1)
    for r in range(slots):
        up = arrived[recv[r]]
        down = arrived[recv[slots + r]]
        out[r] = jnp.where(lane < HALF, down, up)


def shifted(plane, by):
    return pltpu.roll(plane, by % LANES, axis=1)


def half_weights(weights, wide, upper):
    channels, every = weights.shape[1:]
    half = every // 2
    for g in range(9):
        for r in range(3):
            w = weights[3 * g + r]
            wide[g * channels : (g + 1) * channels, r * half : (r + 1) * half] = jnp.where(
                upper, w[:, half:], w[:, :half]
            )


def conv_blocks(blocks, sets, wide, expand):
    channels = wide.shape[0] // 9
    for (row, parts), (rows, stack, prod) in zip(blocks, sets):
        size = rows.shape[0] // 4
        for at, x in parts:
            masked = x * row
            for v in range(4):
                here = pl.multiple_of(v * size + at, channels)
                rows[pl.ds(here, channels), :] = masked[:, v * LANES : (v + 1) * LANES]
    for rows, stack, prod in sets:
        size = rows.shape[0] // 4
        planes = jnp.dot(rows[...], expand[...], preferred_element_type=jnp.float32).astype(jnp.bfloat16)
        for v in range(4):
            for a in range(2):
                at = slice((2 * v + a) * LANES, (2 * v + a + 1) * LANES)
                plane = planes[v * size : (v + 1) * size, a * LANES : (a + 1) * LANES]
                stack[0:size, at] = shifted(plane, 1)
                stack[size : 2 * size, at] = plane
                stack[2 * size : 3 * size, at] = shifted(plane, -1)
    for rows, stack, prod in sets:
        prod[...] = jnp.dot(wide[...], stack[...], preferred_element_type=jnp.float32)
    for rows, stack, prod in sets:
        results = []
        for layer in range(SIDE):
            sums = []
            for q in range(3):
                total = None
                for p in range(3):
                    inside = layer + p - 1
                    if 0 <= inside < SIDE:
                        first = (3 * p + q) * channels
                        part = prod[first : first + channels, inside * LANES : (inside + 1) * LANES]
                        total = part if total is None else total + part
                sums.append(total)
            results.append(sums[1] + shifted(sums[0], PAD) + shifted(sums[2], -PAD))
        yield results


def block_parts(group, step, me, live, occ, xs):
    n = len(xs)
    channels = xs[0].shape[1]
    blocks = []
    for b in range(group):
        row = active_row(occ, step * group + b, live).astype(jnp.bfloat16)
        blocks.append((row, [(mod(me ^ key, n) * channels, x[b]) for key, x in enumerate(xs)]))
    return blocks


def near_kernel(peers, cap, group, place_ref, me_ref, live_ref, nbr, occ, weights, expand, *refs):
    n = len(refs) - 10 - 3 * group
    xs = refs[:n]
    out, send, recv, far_wide, halo_wide, far_expand, far_occ, wide, count, mask = refs[n : n + 10]
    sets = [refs[n + 10 + 3 * b : n + 13 + 3 * b] for b in range(group)]
    me = me_ref[0]
    channels, every = weights.shape[1:]
    send_slots(peers, cap, group, place_ref, nbr, send, count, True)
    arrival_slots((8, 9), peers, cap, group, place_ref, nbr, recv, mask, True)
    half_weights(weights, wide, div(me, n) == 1)
    blocks = block_parts(group, 0, me, live_ref[0], occ, xs)
    for b, results in enumerate(conv_blocks(blocks, sets, wide, expand)):
        for layer, result in enumerate(results):
            out[b, :, layer * LANES : (layer + 1) * LANES] = result
    half_weights(weights, far_wide, div(me, n) == 0)
    for side in range(2):
        for g in range(3):
            for r in range(3):
                halo_wide[side, g * channels : (g + 1) * channels, r * every : (r + 1) * every] = weights[
                    18 * side + 3 * g + r
                ]
    far_expand[...] = expand[...]
    far_occ[...] = occ[...]


def far_kernel(group, me_ref, live_ref, occ, wide, expand, gather, near, *refs):
    n = len(refs) - 4 - 3 * group
    xs = refs[:n]
    out, rim, shell, packed = refs[n : n + 4]
    channels = near.shape[1]
    step = pl.program_id(0)
    me = me_ref[0]

    blocks = block_parts(group, step, me, live_ref[0], occ, xs)
    sets = [refs[n + 4 + 3 * b : n + 7 + 3 * b] for b in range(group)]
    for b, results in enumerate(conv_blocks(blocks, sets, wide, expand)):
        for layer, result in enumerate(results):
            at = slice(layer * LANES, (layer + 1) * LANES)
            total = result + near[step * group + b, :, at]
            out[b, :, at] = total
            if 0 < layer < SIDE - 1:
                packed[b, :, (layer - 1) * LANES : layer * LANES] = total.astype(jnp.bfloat16)
            else:
                side = slice(LANES * (layer > 0), LANES * (layer > 0) + LANES)
                rim[step * group + b, :, side] = total
    picked = jnp.dot(
        packed[...].reshape(group * channels, (SIDE - 2) * LANES),
        gather[...],
        preferred_element_type=jnp.float32,
    )
    shell[pl.ds(step * group, group)] = picked.astype(jnp.bfloat16).reshape(packed.shape[:2] + shell.shape[2:])


def edge_mask(lane, quarter, e):
    return jnp.logical_and((lane >> 5) == quarter, ((lane >> 3) & 3) == e)


def halo_kernel(slots, cap, me_ref, send, wide, expand, gather, shell, base, *refs):
    n = len(refs) - 7
    hs = refs[:n]
    added, faces = refs[n : n + 2]
    rows, stack, prod, packed, edges = refs[n + 2 :]
    channels, every = wide.shape[1] // 3, wide.shape[2] // 3
    me = me_ref[0]
    for r in range(slots):
        for key, h in enumerate(hs):
            at = pl.multiple_of((me ^ key) * channels + r * every, channels)
            rows[pl.ds(at, channels), :] = h[r]
    for r in range(slots):
        planes = jnp.dot(
            rows[r * every : (r + 1) * every, :], expand[...], preferred_element_type=jnp.float32
        ).astype(jnp.bfloat16)
        at = slice(r * LANES, (r + 1) * LANES)
        for side in range(2):
            plane = planes[:, (1 - side) * LANES : (2 - side) * LANES]
            stack[side, 0:every, at] = shifted(plane, 1)
            stack[side, every : 2 * every, at] = plane
            stack[side, 2 * every : 3 * every, at] = shifted(plane, -1)
    for side in range(2):
        prod[side] = jnp.dot(wide[side], stack[side], preferred_element_type=jnp.float32)
    for r in range(slots):
        at = slice(r * LANES, (r + 1) * LANES)
        for side in range(2):
            sums = [prod[side, q * channels : (q + 1) * channels, at] for q in range(3)]
            result = sums[1] + shifted(sums[0], PAD) + shifted(sums[2], -PAD)
            here = slice(side * LANES, (side + 1) * LANES)
            added[r, :, here] = result
            packed[r, :, here] = (base[r, :, here] + result).astype(jnp.bfloat16)
    picked = jnp.dot(packed[...].reshape(slots * channels, 2 * LANES), gather[...], preferred_element_type=jnp.float32)
    for s in range(slots):
        mine = picked[s * channels : (s + 1) * channels].astype(jnp.bfloat16) + shell[s]
        for d in range(2):
            pair = mine[:, d * LANES : (d + 1) * LANES]
            faces[send[(2 * d + 1) * slots + s], :, :HALF] = pair[:, :HALF]
            faces[send[2 * d * slots + s], :, HALF:] = pair[:, HALF:]
        quarter = slice((s & 3) * 4 * SIDE, ((s & 3) + 1) * 4 * SIDE)
        edges[s >> 2, :, quarter] = mine[:, 2 * LANES :][:, quarter]
    size = 2 * cap + slots // 4
    for peer in range(faces.shape[0] // size):
        faces[peer * size + 2 * cap : (peer + 1) * size] = edges[...]


def squeeze_kernel(part, bias, squeeze, base, added, scatter, occ, out, finish_scatter, finish_occ):
    finish_scatter[...] = scatter[...]
    finish_occ[...] = occ[...]
    for n in range(part):
        b = pl.program_id(0) * part + n
        for v in range(4):
            pair = base[n, :, 2 * v * LANES : 2 * (v + 1) * LANES] + bias[...]
            if v in (0, 3):
                extra = added[b, :, LANES * (v > 0) : LANES * (v > 0) + LANES]
                zero = jnp.zeros_like(extra)
                pair = pair + jnp.concatenate([extra, zero] if v == 0 else [zero, extra], axis=1)
            total = None
            for _ in range(3):
                term = pair.astype(jnp.bfloat16)
                pair = pair - term.astype(jnp.float32)
                flat = jnp.dot(term, squeeze[...], preferred_element_type=jnp.float32)
                total = flat if total is None else total + flat
            out[b, :, v * LANES : (v + 1) * LANES] = total


def finish_kernel(slots, part, recv, live_ref, occ, scatter, base, faces, out, shell):
    channels = base.shape[1]
    live = live_ref[0]
    first = pl.program_id(0) * part
    lane = lax.broadcasted_iota(jnp.int32, (channels, LANES), 1)
    for n in range(part):
        r = first + n
        for d in range(2):
            up = faces[recv[2 * d * slots + r]]
            down = faces[recv[(2 * d + 1) * slots + r]]
            shell[n, :, d * LANES : (d + 1) * LANES] = jnp.where(lane < HALF, down, up)
        total = jnp.zeros((channels, LANES), jnp.bfloat16)
        for e in range(4):
            slot = recv[(4 + e) * slots + r]
            total = jnp.where(edge_mask(lane, slot & 3, e), faces[slot >> 2], total)
        shell[n, :, 2 * LANES :] = total
    added = jnp.dot(
        shell[...].reshape(part * channels, 3 * LANES), scatter[...], preferred_element_type=jnp.float32
    )
    for n in range(part):
        summed = base[first + n] + added[n * channels : (n + 1) * channels]
        out[n] = (summed * active_row(occ, first + n, live)).astype(jnp.bfloat16)


def spread(x, axis, near, size):
    have = {0: x}
    bit = near >> 1
    while bit:
        for key in list(have):
            have[key ^ bit] = lax.ppermute(have[key], axis, [(n, n ^ bit) for n in range(size)])
        bit >>= 1
    return [have[key] for key in range(near)]


def spread_direct(x, axis, size):
    return [x] + [lax.ppermute(x, axis, [(n, n ^ key) for n in range(size)]) for key in range(1, size)]


def shards(features, weights, bias, occupancy, live, neighbours):
    slots, channels, voxels = features.shape
    peers = lax.axis_size("blk")
    members = lax.axis_size("ch")
    cap = max(2, 2 * slots // peers)
    every = channels * members
    group = 8 if slots % 8 == 0 else slots
    part = 4
    bf16, f32, i32 = jnp.bfloat16, jnp.float32, jnp.int32
    smem = pl.BlockSpec(memory_space=pltpu.SMEM)
    vmem = pl.BlockSpec(memory_space=pltpu.VMEM)
    resident = lambda x: pltpu.with_memory_space_constraint(x, pltpu.VMEM)
    params = pltpu.CompilerParams(vmem_limit_bytes=VMEM_LIMIT)
    expand, picks, scatter = tables()
    squeeze, middle, outermost = expand.T, picks[LANES:-LANES], np.concatenate([picks[:LANES], picks[-LANES:]])
    expand, scatter, squeeze, middle, outermost = (
        jnp.asarray(t, bf16) for t in (expand, scatter, squeeze, middle, outermost)
    )
    place = lax.axis_index("blk").astype(i32).reshape(1)
    member = lax.axis_index("ch").astype(i32).reshape(1)
    nbr = neighbours.transpose(1, 2, 0)

    corner = pl.BlockSpec((slots, channels, LANES), lambda n: (0, 0, 0))
    corner_last = pl.BlockSpec((slots, channels, LANES), lambda n: (0, 0, voxels // LANES - 1))
    outgoing = pl.pallas_call(
        functools.partial(pack_kernel, peers, cap, slots),
        grid=(1,),
        out_shape=jax.ShapeDtypeStruct((peers * cap, channels, LANES), bf16),
        in_specs=[smem, smem, smem, vmem, corner, corner_last],
        out_specs=vmem,
        scratch_shapes=[pltpu.SMEM((2 * peers,), i32)],
        compiler_params=params,
        name="pack_layers",
    )(place, live, nbr, occupancy, features, features)
    outgoing, shipped = lax.optimization_barrier((outgoing, features))
    half = members // 2
    across = lax.ppermute(shipped, "ch", [(n, n ^ half) for n in range(members)])
    arrived = lax.all_to_all(outgoing, "blk", split_axis=0, concat_axis=0, tiled=True)
    beside = spread(shipped, "ch", half, members)

    per_block = lambda width: pl.BlockSpec((group, channels, width), lambda n: (n, 0, 0))
    some = lambda width: pl.BlockSpec((part, channels, width), lambda n: (n, 0, 0))
    buffers = lambda count: [
        pltpu.VMEM((4 * half * channels, LANES), bf16),
        pltpu.VMEM((3 * half * channels, SIDE * LANES), bf16),
        pltpu.VMEM((9 * channels, SIDE * LANES), f32),
    ] * count
    wide = pltpu.VMEM((9 * channels, 3 * half * channels), bf16)
    near, send, incoming, far_wide, halo_wide, far_expand, far_occ = pl.pallas_call(
        functools.partial(near_kernel, peers, cap, slots),
        out_shape=(
            pltpu.VMEM((slots, channels, SIDE * LANES), f32),
            jax.ShapeDtypeStruct((4 * slots,), i32),
            jax.ShapeDtypeStruct((2 * slots,), i32),
            pltpu.VMEM((9 * channels, 3 * half * channels), bf16),
            pltpu.VMEM((2, 3 * channels, 3 * every), bf16),
            pltpu.VMEM(expand.shape, bf16),
            pltpu.VMEM(occupancy.shape, i32),
        ),
        in_specs=[smem, smem, smem, smem, vmem, vmem, vmem] + [vmem] * half,
        out_specs=(vmem, smem, smem) + (vmem,) * 4,
        scratch_shapes=[wide, pltpu.SMEM((4 * peers,), i32), pltpu.SMEM((2 * peers,), i32)] + buffers(slots),
        compiler_params=params,
        name="convolve_near",
    )(place, member, live, nbr, occupancy, weights, expand, *beside)
    across, near = lax.optimization_barrier((across, near))
    remote = spread(across, "ch", half, members)

    arrived, incoming = lax.optimization_barrier((arrived, incoming))
    layers = pl.pallas_call(
        functools.partial(order_kernel, slots),
        out_shape=pltpu.VMEM((slots, channels, LANES), bf16),
        in_specs=[smem, vmem],
        out_specs=vmem,
        compiler_params=params,
        name="order_layers",
    )(incoming, resident(arrived))
    halo = spread_direct(layers, "ch", members)

    *remote, _ = lax.optimization_barrier((*remote, layers))
    base, rim, shell = pl.pallas_call(
        functools.partial(far_kernel, group),
        grid=(slots // group,),
        out_shape=(
            jax.ShapeDtypeStruct((slots, channels, SIDE * LANES), f32),
            pltpu.VMEM((slots, channels, 2 * LANES), f32),
            pltpu.VMEM((slots, channels, 3 * LANES), bf16),
        ),
        in_specs=[smem, smem, vmem, vmem, vmem, vmem, vmem] + [per_block(voxels)] * half,
        out_specs=(per_block(SIDE * LANES), vmem, vmem),
        scratch_shapes=[
            pltpu.VMEM((group, channels, (SIDE - 2) * LANES), bf16),
        ]
        + buffers(group),
        compiler_params=params,
        name="convolve_far",
    )(
        member, live, resident(far_occ), resident(far_wide), resident(far_expand), middle, resident(near),
        *[resident(x) for x in remote],
    )

    added, faces = pl.pallas_call(
        functools.partial(halo_kernel, slots, cap),
        out_shape=(
            pltpu.VMEM((slots, channels, 2 * LANES), f32),
            pltpu.VMEM((peers * (2 * cap + slots // 4), channels, LANES), bf16),
        ),
        in_specs=[smem, smem, vmem, vmem, vmem, vmem, vmem] + [vmem] * members,
        out_specs=(vmem, vmem),
        scratch_shapes=[
            pltpu.VMEM((slots * every, LANES), bf16),
            pltpu.VMEM((2, 3 * every, slots * LANES), bf16),
            pltpu.VMEM((2, 3 * channels, slots * LANES), f32),
            pltpu.VMEM((slots, channels, 2 * LANES), bf16),
            pltpu.VMEM((slots // 4, channels, LANES), bf16),
        ],
        compiler_params=params,
        name="convolve_halo",
    )(
        member, send, resident(halo_wide), resident(far_expand), outermost, resident(shell), resident(rim),
        *[resident(x) for x in halo],
    )

    faces = lax.all_to_all(faces, "blk", split_axis=0, concat_axis=0, tiled=True)

    base, scatter, occupancy = pl.pallas_call(
        functools.partial(squeeze_kernel, part),
        grid=(slots // part,),
        out_shape=(
            pltpu.VMEM((slots, channels, voxels), f32),
            pltpu.VMEM(scatter.shape, bf16),
            pltpu.VMEM(occupancy.shape, i32),
        ),
        in_specs=[vmem, vmem, some(SIDE * LANES), vmem, vmem, vmem],
        out_specs=(vmem, vmem, vmem),
        compiler_params=params,
        name="squeeze_planes",
    )(bias[:, None], squeeze, base, resident(added), scatter, occupancy)

    recv = pl.pallas_call(
        functools.partial(late_kernel, peers, cap, slots),
        out_shape=jax.ShapeDtypeStruct((8 * slots,), i32),
        in_specs=[smem, smem],
        out_specs=smem,
        scratch_shapes=[pltpu.SMEM((4 * peers,), i32)],
        name="late_tables",
    )(place, nbr)
    return pl.pallas_call(
        functools.partial(finish_kernel, slots, group),
        grid=(slots // group,),
        out_shape=jax.ShapeDtypeStruct((slots, channels, voxels), bf16),
        in_specs=[smem, smem] + [vmem] * 4,
        out_specs=per_block(voxels),
        scratch_shapes=[pltpu.VMEM((group, channels, 3 * LANES), bf16)],
        compiler_params=params,
        name="finish",
    )(
        recv, live, resident(occupancy), resident(scatter), resident(base), resident(faces),
    )


def solution(mesh):
    in_specs = (P("blk", "ch", None), P(None, "ch", None), P("ch"), P("blk", None), P("blk"), P())
    out_specs = P("blk", "ch", None)
    return jax.shard_map(shards, mesh=mesh, in_specs=in_specs, out_specs=out_specs, check_vma=False)
```

```python
import functools

import jax
import jax.numpy as jnp
import numpy as np
from jax import lax
from jax.experimental import pallas as pl
from jax.experimental.pallas import tpu as pltpu
from jax.sharding import PartitionSpec as P

SIDE = 8
PAD = SIDE + 2
LANES = 128
HALF = SIDE * SIDE
VMEM_LIMIT = 57 * 1024 * 1024

FACES = [(1, 0), (1, 1), (2, 0), (2, 1)]
EDGES = [(0, 0), (0, 1), (1, 0), (1, 1)]


def outer(q):
    return PAD - 1 if q == 0 else 0


def inner(q):
    return 0 if q == 0 else SIDE - 1


@functools.lru_cache(None)
def tables():
    expand = np.zeros((LANES, 2 * LANES), np.float32)
    for a in range(2):
        for j in range(SIDE):
            for k in range(SIDE):
                expand[a * HALF + j * SIDE + k, a * LANES + (j + 1) * PAD + k + 1] = 1
    gather = np.zeros((SIDE * LANES, 3 * LANES), np.float32)
    scatter = np.zeros((3 * LANES, SIDE * HALF), np.float32)
    for i in range(SIDE):
        for d, q in FACES:
            for a in range(SIDE):
                lane = (d - 1) * LANES + (1 - q) * HALF + i * SIDE + a
                if d == 1:
                    source, target = outer(q) * PAD + a + 1, inner(q) * SIDE + a
                else:
                    source, target = (a + 1) * PAD + outer(q), a * SIDE + inner(q)
                gather[i * LANES + source, lane] = 1
                scatter[lane, i * HALF + target] = 1
        for quarter in range(4):
            for e, (qj, qk) in enumerate(EDGES):
                lane = 2 * LANES + quarter * 4 * SIDE + e * SIDE + i
                gather[i * LANES + outer(qj) * PAD + outer(qk), lane] = 1
                scatter[lane, i * HALF + inner(qj) * SIDE + inner(qk)] = 1
    return expand, gather, scatter


def div(value, size):
    return value >> (size.bit_length() - 1) if size & (size - 1) == 0 else lax.div(value, size)


def mod(value, size):
    return value & (size - 1) if size & (size - 1) == 0 else lax.rem(value, size)


def popcount(x):
    x = x - ((x >> 1) & 0x55555555)
    x = (x & 0x33333333) + ((x >> 2) & 0x33333333)
    x = (x + (x >> 4)) & 0x0F0F0F0F
    x = x + (x >> 8)
    return (x + (x >> 16)) & 0x3F


def each(size, step, unrolled):
    if unrolled:
        for n in range(size):
            step(n, 0)
    else:
        lax.fori_loop(0, size, step, 0)


def clear(ref, size, unrolled=False):
    def step(n, _):
        ref[n] = 0
        return 0

    each(size, step, unrolled)


def slot_of(kind, peer, place, cap, slots):
    if kind < 4:
        return peer * (2 * cap + slots // 4) + (FACES[kind][0] - 1) * cap + place
    return peer * cap + place


def neighbour(nbr, b, d, q):
    return nbr[d, q, b]


def dest(nbr, b, kind):
    return neighbour(nbr, b, *FACES[kind])


def source(nbr, r, kind):
    if kind >= 8:
        return neighbour(nbr, r, 0, 1 - (kind - 8))
    if kind < 4:
        d, q = FACES[kind]
        return neighbour(nbr, r, d, 1 - q)
    qj, qk = EDGES[kind - 4]
    return neighbour(nbr, neighbour(nbr, r, 2, 1 - qk), 1, 1 - qj)


def send_slots(peers, cap, slots, me_ref, nbr, send, count, unrolled):
    first = me_ref[0] * slots
    clear(count, 4 * peers, unrolled)

    def place_of(s, _):
        for kind in range(4):
            peer = div(dest(nbr, first + s, kind), slots)
            place = count[kind * peers + peer]
            count[kind * peers + peer] = place + 1
            send[kind * slots + s] = slot_of(kind, peer, place, cap, slots)
        return 0

    each(slots, place_of, unrolled)


def arrival_slots(kinds, peers, cap, slots, me_ref, nbr, recv, mask, unrolled=False):
    first = me_ref[0] * slots
    clear(mask, len(kinds) * peers, unrolled)

    def gather(s, _):
        for n, kind in enumerate(kinds):
            b = source(nbr, first + s, kind)
            at = n * peers + div(b, slots)
            mask[at] = mask[at] | (1 << mod(b, slots))
        return 0

    each(slots, gather, unrolled)

    def rank(r, _):
        for n, kind in enumerate(kinds):
            b = source(nbr, first + r, kind)
            peer = div(b, slots)
            before = popcount(mask[n * peers + peer] & ((1 << mod(b, slots)) - 1))
            recv[n * slots + r] = slot_of(kind, peer, before, cap, slots)
        return 0

    each(slots, rank, unrolled)


def late_kernel(peers, cap, slots, me_ref, nbr, recv, mask):
    arrival_slots(range(4), peers, cap, slots, me_ref, nbr, recv, mask)
    me = me_ref[0]

    def place_of(r, _):
        for kind in range(4, 8):
            b = source(nbr, me * slots + r, kind)
            row = div(b, slots) * (2 * cap + slots // 4) + 2 * cap
            recv[kind * slots + r] = row * 4 + mod(b, slots)
        return 0

    lax.fori_loop(0, slots, place_of, 0)


def active_row(occ_ref, s, live):
    return occ_ref[pl.ds(s, 1), :].astype(jnp.float32) * (s < live).astype(jnp.float32)


def pack_kernel(peers, cap, slots, me_ref, live_ref, nbr, occ, low, high, out, count):
    first = me_ref[0] * slots
    live = live_ref[0]
    clear(count, 2 * peers)
    for s in range(slots):
        row = active_row(occ, s, live).astype(jnp.bfloat16)
        for q in range(2):
            peer = div(neighbour(nbr, first + s, 0, q), slots)
            place = count[q * peers + peer]
            count[q * peers + peer] = place + 1
            half = slice(0, HALF) if q == 1 else slice(HALF, LANES)
            face = low if q == 1 else high
            lanes = row[:, :LANES] if q == 1 else row[:, -LANES:]
            out[peer * cap + place, :, half] = (face[s] * lanes)[:, half]


def order_kernel(slots, recv, arrived, out):
    lane = lax.broadcasted_iota(jnp.int32, arrived.shape[1:], 1)
    for r in range(slots):
        up = arrived[recv[r]]
        down = arrived[recv[slots + r]]
        out[r] = jnp.where(lane < HALF, down, up)


def shifted(plane, by):
    return pltpu.roll(plane, by % LANES, axis=1)


def half_weights(weights, wide, upper):
    channels, every = weights.shape[1:]
    half = every // 2
    for g in range(9):
        for r in range(3):
            w = weights[3 * g + r]
            wide[g * channels : (g + 1) * channels, r * half : (r + 1) * half] = jnp.where(
                upper, w[:, half:], w[:, :half]
            )


def conv_blocks(blocks, sets, wide, expand):
    channels = wide.shape[0] // 9
    for (row, parts), (rows, stack, prod) in zip(blocks, sets):
        size = rows.shape[0] // 4
        for at, x in parts:
            masked = x * row
            for v in range(4):
                here = pl.multiple_of(v * size + at, channels)
                rows[pl.ds(here, channels), :] = masked[:, v * LANES : (v + 1) * LANES]
    for rows, stack, prod in sets:
        size = rows.shape[0] // 4
        planes = jnp.dot(rows[...], expand[...], preferred_element_type=jnp.float32).astype(jnp.bfloat16)
        for v in range(4):
            for a in range(2):
                at = slice((2 * v + a) * LANES, (2 * v + a + 1) * LANES)
                plane = planes[v * size : (v + 1) * size, a * LANES : (a + 1) * LANES]
                stack[0:size, at] = shifted(plane, 1)
                stack[size : 2 * size, at] = plane
                stack[2 * size : 3 * size, at] = shifted(plane, -1)
    for rows, stack, prod in sets:
        prod[...] = jnp.dot(wide[...], stack[...], preferred_element_type=jnp.float32)
    for rows, stack, prod in sets:
        results = []
        for layer in range(SIDE):
            sums = []
            for q in range(3):
                total = None
                for p in range(3):
                    inside = layer + p - 1
                    if 0 <= inside < SIDE:
                        first = (3 * p + q) * channels
                        part = prod[first : first + channels, inside * LANES : (inside + 1) * LANES]
                        total = part if total is None else total + part
                sums.append(total)
            results.append(sums[1] + shifted(sums[0], PAD) + shifted(sums[2], -PAD))
        yield results


def block_parts(group, step, me, live, occ, xs):
    n = len(xs)
    channels = xs[0].shape[1]
    blocks = []
    for b in range(group):
        row = active_row(occ, step * group + b, live).astype(jnp.bfloat16)
        blocks.append((row, [(mod(me ^ key, n) * channels, x[b]) for key, x in enumerate(xs)]))
    return blocks


def near_kernel(peers, cap, group, place_ref, me_ref, live_ref, nbr, occ, weights, expand, *refs):
    n = len(refs) - 10 - 3 * group
    xs = refs[:n]
    out, send, recv, far_wide, halo_wide, far_expand, far_occ, wide, count, mask = refs[n : n + 10]
    sets = [refs[n + 10 + 3 * b : n + 13 + 3 * b] for b in range(group)]
    me = me_ref[0]
    channels, every = weights.shape[1:]
    send_slots(peers, cap, group, place_ref, nbr, send, count, True)
    arrival_slots((8, 9), peers, cap, group, place_ref, nbr, recv, mask, True)
    half_weights(weights, wide, div(me, n) == 1)
    blocks = block_parts(group, 0, me, live_ref[0], occ, xs)
    for b, results in enumerate(conv_blocks(blocks, sets, wide, expand)):
        for layer, result in enumerate(results):
            out[b, :, layer * LANES : (layer + 1) * LANES] = result
    half_weights(weights, far_wide, div(me, n) == 0)
    for side in range(2):
        for g in range(3):
            for r in range(3):
                halo_wide[side, g * channels : (g + 1) * channels, r * every : (r + 1) * every] = weights[
                    18 * side + 3 * g + r
                ]
    far_expand[...] = expand[...]
    far_occ[...] = occ[...]


def far_kernel(group, me_ref, live_ref, occ, wide, expand, gather, near, *refs):
    n = len(refs) - 4 - 3 * group
    xs = refs[:n]
    out, rim, shell, packed = refs[n : n + 4]
    channels = near.shape[1]
    step = pl.program_id(0)
    me = me_ref[0]

    blocks = block_parts(group, step, me, live_ref[0], occ, xs)
    sets = [refs[n + 4 + 3 * b : n + 7 + 3 * b] for b in range(group)]
    for b, results in enumerate(conv_blocks(blocks, sets, wide, expand)):
        for layer, result in enumerate(results):
            at = slice(layer * LANES, (layer + 1) * LANES)
            total = result + near[step * group + b, :, at]
            out[b, :, at] = total
            if 0 < layer < SIDE - 1:
                packed[b, :, (layer - 1) * LANES : layer * LANES] = total.astype(jnp.bfloat16)
            else:
                side = slice(LANES * (layer > 0), LANES * (layer > 0) + LANES)
                rim[step * group + b, :, side] = total
    picked = jnp.dot(
        packed[...].reshape(group * channels, (SIDE - 2) * LANES),
        gather[...],
        preferred_element_type=jnp.float32,
    )
    shell[pl.ds(step * group, group)] = picked.astype(jnp.bfloat16).reshape(packed.shape[:2] + shell.shape[2:])


def edge_mask(lane, quarter, e):
    return jnp.logical_and((lane >> 5) == quarter, ((lane >> 3) & 3) == e)


def halo_kernel(slots, cap, me_ref, send, wide, expand, gather, shell, base, *refs):
    n = len(refs) - 7
    hs = refs[:n]
    added, faces = refs[n : n + 2]
    rows, stack, prod, packed, edges = refs[n + 2 :]
    channels, every = wide.shape[1] // 3, wide.shape[2] // 3
    me = me_ref[0]
    for r in range(slots):
        for key, h in enumerate(hs):
            at = pl.multiple_of((me ^ key) * channels + r * every, channels)
            rows[pl.ds(at, channels), :] = h[r]
    for r in range(slots):
        planes = jnp.dot(
            rows[r * every : (r + 1) * every, :], expand[...], preferred_element_type=jnp.float32
        ).astype(jnp.bfloat16)
        at = slice(r * LANES, (r + 1) * LANES)
        for side in range(2):
            plane = planes[:, (1 - side) * LANES : (2 - side) * LANES]
            stack[side, 0:every, at] = shifted(plane, 1)
            stack[side, every : 2 * every, at] = plane
            stack[side, 2 * every : 3 * every, at] = shifted(plane, -1)
    for side in range(2):
        prod[side] = jnp.dot(wide[side], stack[side], preferred_element_type=jnp.float32)
    for r in range(slots):
        at = slice(r * LANES, (r + 1) * LANES)
        for side in range(2):
            sums = [prod[side, q * channels : (q + 1) * channels, at] for q in range(3)]
            result = sums[1] + shifted(sums[0], PAD) + shifted(sums[2], -PAD)
            here = slice(side * LANES, (side + 1) * LANES)
            added[r, :, here] = result
            packed[r, :, here] = (base[r, :, here] + result).astype(jnp.bfloat16)
    picked = jnp.dot(packed[...].reshape(slots * channels, 2 * LANES), gather[...], preferred_element_type=jnp.float32)
    for s in range(slots):
        mine = picked[s * channels : (s + 1) * channels].astype(jnp.bfloat16) + shell[s]
        for d in range(2):
            pair = mine[:, d * LANES : (d + 1) * LANES]
            faces[send[(2 * d + 1) * slots + s], :, :HALF] = pair[:, :HALF]
            faces[send[2 * d * slots + s], :, HALF:] = pair[:, HALF:]
        quarter = slice((s & 3) * 4 * SIDE, ((s & 3) + 1) * 4 * SIDE)
        edges[s >> 2, :, quarter] = mine[:, 2 * LANES :][:, quarter]
    size = 2 * cap + slots // 4
    for peer in range(faces.shape[0] // size):
        faces[peer * size + 2 * cap : (peer + 1) * size] = edges[...]


def squeeze_kernel(part, bias, squeeze, base, added, scatter, occ, out, finish_scatter, finish_occ):
    finish_scatter[...] = scatter[...]
    finish_occ[...] = occ[...]
    for n in range(part):
        b = pl.program_id(0) * part + n
        for v in range(4):
            pair = base[n, :, 2 * v * LANES : 2 * (v + 1) * LANES] + bias[...]
            if v in (0, 3):
                extra = added[b, :, LANES * (v > 0) : LANES * (v > 0) + LANES]
                zero = jnp.zeros_like(extra)
                pair = pair + jnp.concatenate([extra, zero] if v == 0 else [zero, extra], axis=1)
            total = None
            for _ in range(3):
                term = pair.astype(jnp.bfloat16)
                pair = pair - term.astype(jnp.float32)
                flat = jnp.dot(term, squeeze[...], preferred_element_type=jnp.float32)
                total = flat if total is None else total + flat
            out[b, :, v * LANES : (v + 1) * LANES] = total


def finish_kernel(slots, part, recv, live_ref, occ, scatter, base, faces, out, shell):
    channels = base.shape[1]
    live = live_ref[0]
    first = pl.program_id(0) * part
    lane = lax.broadcasted_iota(jnp.int32, (channels, LANES), 1)
    for n in range(part):
        r = first + n
        for d in range(2):
            up = faces[recv[2 * d * slots + r]]
            down = faces[recv[(2 * d + 1) * slots + r]]
            shell[n, :, d * LANES : (d + 1) * LANES] = jnp.where(lane < HALF, down, up)
        total = jnp.zeros((channels, LANES), jnp.bfloat16)
        for e in range(4):
            slot = recv[(4 + e) * slots + r]
            total = jnp.where(edge_mask(lane, slot & 3, e), faces[slot >> 2], total)
        shell[n, :, 2 * LANES :] = total
    added = jnp.dot(
        shell[...].reshape(part * channels, 3 * LANES), scatter[...], preferred_element_type=jnp.float32
    )
    for n in range(part):
        summed = base[first + n] + added[n * channels : (n + 1) * channels]
        out[n] = (summed * active_row(occ, first + n, live)).astype(jnp.bfloat16)


def spread(x, axis, near, size):
    have = {0: x}
    bit = near >> 1
    while bit:
        for key in list(have):
            have[key ^ bit] = lax.ppermute(have[key], axis, [(n, n ^ bit) for n in range(size)])
        bit >>= 1
    return [have[key] for key in range(near)]


def spread_direct(x, axis, size):
    return [x] + [lax.ppermute(x, axis, [(n, n ^ key) for n in range(size)]) for key in range(1, size)]


def shards(features, weights, bias, occupancy, live, neighbours):
    slots, channels, voxels = features.shape
    peers = lax.axis_size("blk")
    members = lax.axis_size("ch")
    cap = max(2, 2 * slots // peers)
    every = channels * members
    group = slots
    part = 4
    bf16, f32, i32 = jnp.bfloat16, jnp.float32, jnp.int32
    smem = pl.BlockSpec(memory_space=pltpu.SMEM)
    vmem = pl.BlockSpec(memory_space=pltpu.VMEM)
    resident = lambda x: pltpu.with_memory_space_constraint(x, pltpu.VMEM)
    params = pltpu.CompilerParams(vmem_limit_bytes=VMEM_LIMIT)
    expand, picks, scatter = tables()
    squeeze, middle, outermost = expand.T, picks[LANES:-LANES], np.concatenate([picks[:LANES], picks[-LANES:]])
    expand, scatter, squeeze, middle, outermost = (
        jnp.asarray(t, bf16) for t in (expand, scatter, squeeze, middle, outermost)
    )
    place = lax.axis_index("blk").astype(i32).reshape(1)
    member = lax.axis_index("ch").astype(i32).reshape(1)
    nbr = neighbours.transpose(1, 2, 0)

    corner = pl.BlockSpec((slots, channels, LANES), lambda n: (0, 0, 0))
    corner_last = pl.BlockSpec((slots, channels, LANES), lambda n: (0, 0, voxels // LANES - 1))
    outgoing = pl.pallas_call(
        functools.partial(pack_kernel, peers, cap, slots),
        grid=(1,),
        out_shape=jax.ShapeDtypeStruct((peers * cap, channels, LANES), bf16),
        in_specs=[smem, smem, smem, vmem, corner, corner_last],
        out_specs=vmem,
        scratch_shapes=[pltpu.SMEM((2 * peers,), i32)],
        compiler_params=params,
        name="pack_layers",
    )(place, live, nbr, occupancy, features, features)
    outgoing, shipped = lax.optimization_barrier((outgoing, features))
    half = members // 2
    across = lax.ppermute(shipped, "ch", [(n, n ^ half) for n in range(members)])
    arrived = lax.all_to_all(outgoing, "blk", split_axis=0, concat_axis=0, tiled=True)
    beside = spread(shipped, "ch", half, members)

    per_block = lambda width: pl.BlockSpec((group, channels, width), lambda n: (n, 0, 0))
    some = lambda width: pl.BlockSpec((part, channels, width), lambda n: (n, 0, 0))
    buffers = lambda count: [
        pltpu.VMEM((4 * half * channels, LANES), bf16),
        pltpu.VMEM((3 * half * channels, SIDE * LANES), bf16),
        pltpu.VMEM((9 * channels, SIDE * LANES), f32),
    ] * count
    wide = pltpu.VMEM((9 * channels, 3 * half * channels), bf16)
    near, send, incoming, far_wide, halo_wide, far_expand, far_occ = pl.pallas_call(
        functools.partial(near_kernel, peers, cap, slots),
        out_shape=(
            pltpu.VMEM((slots, channels, SIDE * LANES), f32),
            jax.ShapeDtypeStruct((4 * slots,), i32),
            jax.ShapeDtypeStruct((2 * slots,), i32),
            pltpu.VMEM((9 * channels, 3 * half * channels), bf16),
            pltpu.VMEM((2, 3 * channels, 3 * every), bf16),
            pltpu.VMEM(expand.shape, bf16),
            pltpu.VMEM(occupancy.shape, i32),
        ),
        in_specs=[smem, smem, smem, smem, vmem, vmem, vmem] + [vmem] * half,
        out_specs=(vmem, smem, smem) + (vmem,) * 4,
        scratch_shapes=[wide, pltpu.SMEM((4 * peers,), i32), pltpu.SMEM((2 * peers,), i32)] + buffers(slots),
        compiler_params=params,
        name="convolve_near",
    )(place, member, live, nbr, occupancy, weights, expand, *beside)
    across, near = lax.optimization_barrier((across, near))
    remote = spread(across, "ch", half, members)

    arrived, incoming = lax.optimization_barrier((arrived, incoming))
    layers = pl.pallas_call(
        functools.partial(order_kernel, slots),
        out_shape=pltpu.VMEM((slots, channels, LANES), bf16),
        in_specs=[smem, vmem],
        out_specs=vmem,
        compiler_params=params,
        name="order_layers",
    )(incoming, resident(arrived))
    halo = spread_direct(layers, "ch", members)

    *remote, _ = lax.optimization_barrier((*remote, layers))
    base, rim, shell = pl.pallas_call(
        functools.partial(far_kernel, group),
        grid=(slots // group,),
        out_shape=(
            jax.ShapeDtypeStruct((slots, channels, SIDE * LANES), f32),
            pltpu.VMEM((slots, channels, 2 * LANES), f32),
            pltpu.VMEM((slots, channels, 3 * LANES), bf16),
        ),
        in_specs=[smem, smem, vmem, vmem, vmem, vmem, vmem] + [per_block(voxels)] * half,
        out_specs=(per_block(SIDE * LANES), vmem, vmem),
        scratch_shapes=[
            pltpu.VMEM((group, channels, (SIDE - 2) * LANES), bf16),
        ]
        + buffers(group),
        compiler_params=params,
        name="convolve_far",
    )(
        member, live, resident(far_occ), resident(far_wide), resident(far_expand), middle, resident(near),
        *[resident(x) for x in remote],
    )

    added, faces = pl.pallas_call(
        functools.partial(halo_kernel, slots, cap),
        out_shape=(
            pltpu.VMEM((slots, channels, 2 * LANES), f32),
            pltpu.VMEM((peers * (2 * cap + slots // 4), channels, LANES), bf16),
        ),
        in_specs=[smem, smem, vmem, vmem, vmem, vmem, vmem] + [vmem] * members,
        out_specs=(vmem, vmem),
        scratch_shapes=[
            pltpu.VMEM((slots * every, LANES), bf16),
            pltpu.VMEM((2, 3 * every, slots * LANES), bf16),
            pltpu.VMEM((2, 3 * channels, slots * LANES), f32),
            pltpu.VMEM((slots, channels, 2 * LANES), bf16),
            pltpu.VMEM((slots // 4, channels, LANES), bf16),
        ],
        compiler_params=params,
        name="convolve_halo",
    )(
        member, send, resident(halo_wide), resident(far_expand), outermost, resident(shell), resident(rim),
        *[resident(x) for x in halo],
    )

    faces = lax.all_to_all(faces, "blk", split_axis=0, concat_axis=0, tiled=True)

    base, scatter, occupancy = pl.pallas_call(
        functools.partial(squeeze_kernel, part),
        grid=(slots // part,),
        out_shape=(
            pltpu.VMEM((slots, channels, voxels), f32),
            pltpu.VMEM(scatter.shape, bf16),
            pltpu.VMEM(occupancy.shape, i32),
        ),
        in_specs=[vmem, vmem, some(SIDE * LANES), vmem, vmem, vmem],
        out_specs=(vmem, vmem, vmem),
        compiler_params=params,
        name="squeeze_planes",
    )(bias[:, None], squeeze, base, resident(added), scatter, occupancy)

    recv = pl.pallas_call(
        functools.partial(late_kernel, peers, cap, slots),
        out_shape=jax.ShapeDtypeStruct((8 * slots,), i32),
        in_specs=[smem, smem],
        out_specs=smem,
        scratch_shapes=[pltpu.SMEM((4 * peers,), i32)],
        name="late_tables",
    )(place, nbr)
    return pl.pallas_call(
        functools.partial(finish_kernel, slots, group),
        grid=(slots // group,),
        out_shape=jax.ShapeDtypeStruct((slots, channels, voxels), bf16),
        in_specs=[smem, smem] + [vmem] * 4,
        out_specs=per_block(voxels),
        scratch_shapes=[pltpu.VMEM((group, channels, 3 * LANES), bf16)],
        compiler_params=params,
        name="finish",
    )(
        recv, live, resident(occupancy), resident(scatter), resident(base), resident(faces),
    )


def solution(mesh):
    in_specs = (P("blk", "ch", None), P(None, "ch", None), P("ch"), P("blk", None), P("blk"), P())
    out_specs = P("blk", "ch", None)
    return jax.shard_map(shards, mesh=mesh, in_specs=in_specs, out_specs=out_specs, check_vma=False)
```
